32 devices in a mesh: dp: 8 (over y, x, core), mp: 4 (over z).
Axes of the slice: x: 2, y: 2, z: 4, core: 2. Of those that a mesh axis runs over, the one named last changes fastest.
Arguments:
- patches: bfloat16 [1024, 6144], P('dp', 'mp'), may hold values from -64 to 64
- send_start: int32 [8, 8], P('dp'), may hold values from 0 to 128, as said below
- run_length: int32 [8, 8], P('dp'), may hold values from 0 to 32, as said below
- slot_start: int32 [8, 8], P('dp'), may hold values from 0 to 128, as said below
- image_ids: int32 [8, 128], P('dp'), may hold values from 0 to 7, never falling along the last dimension, each value on 1 to 32 neighbouring positions
- norm_gain: float32 [6144], replicated, may hold values from 0.1 to 1.9
- qkv_weight: bfloat16 [6144, 3, 4096], P('dp', None, 'mp'), may hold values from -0.078125 to 0.078125
- query_gain: float32 [128], replicated, may hold values from 0.1 to 1.9
- key_gain: float32 [128], replicated, may hold values from 0.1 to 1.9
- out_weight: bfloat16 [4096, 6144], P('mp'), may hold values from -0.09375 to 0.09375
Outputs:
- packed: bfloat16 [1024, 6144], P('dp', 'mp')
- attended: bfloat16 [1024, 6144], P('dp', 'mp')
The draws below stay inside these ranges and needn't reach their ends.
Inputs may be any that keep to these rules, and one draw needn't show every extreme that they name: `run_length`: every source's runs sum to 128 and every pack's runs sum to 128; the longest run is exactly 32. `send_start`: the runs of one source device do not intersect and cover its 128 rows. `slot_start`: the runs into one pack do not intersect and fill its 128 slots. `image_ids`: image numbers never fall along a pack; equal numbers mark one image.
All inputs are finite; a program needn't handle non-finite values.
Results may differ from the reference program's by a relative error of at most 0.011.
Values may be sent and summed in bfloat16 or wider, within the bound.
A program may use at most 128 MiB of HBM per device.

```python
import math
import jax
import jax.numpy as jnp
import numpy as np
from jax import lax

D = 6144
HEADS = 32
HS = 128
PACK = 128
PACKS = 8
TOKENS = 1024
CAP = 32
IMAGES = 8
IMG_MOST = 32
N_MP = 4


def ordered_starts(key_order, run_table):
    row_count = run_table.shape[0]
    rank_draw = jax.vmap(lambda subkey: jax.random.permutation(subkey, row_count))(jax.random.split(key_order, row_count)).astype(jnp.int32)
    sort_key = jnp.where(run_table == 0, rank_draw + row_count, rank_draw)
    visit_order = jnp.argsort(sort_key, axis=1, stable=True).astype(jnp.int32)
    ordered = jnp.take_along_axis(run_table, visit_order, axis=1)
    starts = jnp.cumsum(ordered, axis=1) - ordered
    position = jnp.argsort(visit_order, axis=1, stable=True).astype(jnp.int32)
    return jnp.take_along_axis(starts, position, axis=1).astype(jnp.int32)


def pack_plan(key):
    mean_run = PACK // PACKS
    half_count = PACKS // 2
    excess = jax.random.randint(jax.random.fold_in(key, 11), (half_count,), -mean_run, mean_run + 1).astype(jnp.int32)
    excess = excess.at[0].set(mean_run)
    profile = jnp.concatenate([mean_run + excess, mean_run - excess]).astype(jnp.int32)
    pack_perm = jax.random.permutation(jax.random.fold_in(key, 12), PACKS).astype(jnp.int32)
    source_perm = jax.random.permutation(jax.random.fold_in(key, 13), PACKS).astype(jnp.int32)
    run_table = profile[(source_perm[:, None] + pack_perm[None, :]) % PACKS]
    send_table = ordered_starts(jax.random.fold_in(key, 14), run_table)
    slot_table = ordered_starts(jax.random.fold_in(key, 15), jnp.transpose(run_table))
    return (send_table, run_table.astype(jnp.int32), slot_table)


def draw_send_start(key, part):
    return pack_plan(key)[0]


def draw_run_length(key, part):
    return pack_plan(key)[1]


def draw_slot_start(key, part):
    return pack_plan(key)[2]


def draw_patches(key, part):
    row_scale = jnp.exp(jax.random.uniform(jax.random.fold_in(key, 21), (TOKENS, 1), minval=-1.15, maxval=1.15))
    base = jnp.clip(jax.random.normal(jax.random.fold_in(key, 22), (TOKENS, D)), -6.0, 6.0)
    column_scale = jnp.exp(jax.random.uniform(jax.random.fold_in(key, 23), (1, D), minval=-1.15, maxval=1.15))
    return (base * row_scale * column_scale).astype(jnp.bfloat16)


def block_levels(rng, extent, cuts, smallest, top_value):
    gain = 1.0
    for dim, parts in cuts:
        heights = jax.random.uniform(jax.random.fold_in(jax.random.fold_in(rng, 6), dim), (parts,), jnp.float32, smallest / len(cuts), top_value / len(cuts))
        gain = gain * jnp.repeat(jnp.exp(heights), extent[dim] // parts).reshape((-1,) + (1,) * (len(extent) - 1 - dim))
    return gain


def split_up(count, total, most, skew):
    loads = [(1 << 20) // math.isqrt(standing ** skew) + 1 for standing in range(2, count + 1)]
    spare, holding = total - most - (count - 1), [1] * (count - 1)
    while spare > 0:
        candidates = [i for i in range(count - 1) if holding[i] < most]
        whole, budget = sum([loads[i] for i in candidates]), spare
        for i in candidates:
            more = min(most - holding[i], max(1, budget * loads[i] // whole), spare)
            holding[i] = holding[i] + more
            spare = spare - more
    return np.array([most] + holding)


def uneven(rng, amount, total, bound, lean):
    if amount == 2:
        one = jax.random.randint(rng, (), max(1, total - bound), min(bound, total - 1) + 1)
        return jnp.stack([one, total - one])
    tallies = jnp.asarray(split_up(amount, total, bound, lean), jnp.int32)
    couples = (amount - 1) // 2
    giver, taker = tallies[1:1 + 2 * couples:2], tallies[2:2 + 2 * couples:2]
    slack = jnp.minimum(giver - 1, bound - taker)
    shifted = jax.random.randint(jax.random.fold_in(rng, 1), (couples,), 0, 1 << 20) % (slack + 1)
    tallies = tallies.at[1:1 + 2 * couples:2].set(giver - shifted).at[2:2 + 2 * couples:2].set(taker + shifted)
    return tallies[jax.random.permutation(jax.random.fold_in(rng, 2), amount)]


def centred(key, shape, deviation, most, pieces=(), kind=jnp.bfloat16):
    loudness = block_levels(key, shape, pieces, -0.22, 0.18) if pieces else 1.0
    array = jax.random.normal(key, shape, jnp.float32) * deviation * loudness
    return jnp.minimum(jnp.maximum(array, -most), most).astype(kind)


def setup_inputs(seed: int = 0) -> dict:
    key_list = jax.random.split(jax.random.key(seed), 11)
    patches = draw_patches(jax.random.fold_in(key_list[10], 71), 0)
    send_start = draw_send_start(jax.random.fold_in(key_list[10], 71), 0)
    run_length = draw_run_length(jax.random.fold_in(key_list[10], 71), 0)
    slot_start = draw_slot_start(jax.random.fold_in(key_list[10], 71), 0)
    image_ids = jax.vmap(lambda own: jnp.searchsorted(jnp.cumsum(uneven(own, IMAGES, PACK, IMG_MOST, 2)), jnp.arange(PACK), side="right"))(jax.random.split(key_list[4], PACKS)).reshape((PACKS, PACK)).astype(jnp.int32)
    norm_gain = jnp.clip(1.0 + 0.18 * jax.random.normal(key_list[5], (D,), jnp.float32), 0.1, 1.9)
    qkv_weight = centred(key_list[6], (D, 3, HEADS * HS), D ** -0.5, 0.078125, ((0, 8), (2, 4)))
    query_gain = jnp.clip(1.0 + 0.18 * jax.random.normal(key_list[7], (HS,), jnp.float32), 0.1, 1.9)
    key_gain = jnp.clip(1.0 + 0.18 * jax.random.normal(key_list[8], (HS,), jnp.float32), 0.1, 1.9)
    out_weight = centred(key_list[9], (HEADS * HS, D), (HEADS * HS) ** -0.5, 0.09375, ((0, 4),))
    return dict(patches=patches, send_start=send_start, run_length=run_length, slot_start=slot_start, image_ids=image_ids, norm_gain=norm_gain, qkv_weight=qkv_weight, query_gain=query_gain, key_gain=key_gain, out_weight=out_weight)


epsilon = 1e-06

def row_norm(values, scales):
    middle = lax.optimization_barrier(jnp.mean(values, axis=-1, keepdims=True))
    spread = lax.optimization_barrier(jnp.mean(values * values, axis=-1, keepdims=True)) - middle * middle
    return (values - middle) * lax.rsqrt(spread + epsilon) * scales

def reference(patches, send_start, run_length, slot_start, image_ids, norm_gain, qkv_weight, query_gain, key_gain, out_weight):
    source = jnp.arange(PACKS, dtype=jnp.int32)[:, None, None]
    target = jnp.arange(PACKS, dtype=jnp.int32)[None, :, None]
    within = jnp.arange(CAP, dtype=jnp.int32)[None, None, :]
    source_rows = jnp.clip(source * PACK + send_start[:, :, None] + within, 0, TOKENS - 1)
    dest_rows = target * PACK + jnp.transpose(slot_start)[:, :, None] + within
    dest_rows = jnp.where(within < run_length[:, :, None], dest_rows, TOKENS)
    packed = jnp.zeros_like(patches).at[dest_rows.reshape(-1)].set(patches[source_rows.reshape(-1)], mode='drop')
    flat_weight = qkv_weight.reshape(D, 3 * HEADS * HS)
    out_groups = out_weight.astype(jnp.float32).reshape(N_MP, HEADS * HS // N_MP, D)

    def one_pack(inputs):
        pack_rows, image_of = inputs
        normed = row_norm(pack_rows.astype(jnp.float32), norm_gain).astype(jnp.bfloat16)
        projected = jnp.dot(normed, flat_weight, preferred_element_type=jnp.float32).reshape(PACK, 3, HEADS, HS)
        queries = row_norm(projected[:, 0], query_gain).astype(jnp.bfloat16)
        key_rows = row_norm(projected[:, 1], key_gain).astype(jnp.bfloat16)
        values = projected[:, 2].astype(jnp.bfloat16)
        scores = jnp.einsum('qhd,khd->hqk', queries.astype(jnp.float32), key_rows.astype(jnp.float32)) * HS ** (-0.5)
        same_image = image_of[:, None] == image_of[None, :]
        weights_raw = jnp.where(same_image[None], jnp.exp(scores), 0.0)
        totals = lax.optimization_barrier(jnp.sum(weights_raw, axis=-1, keepdims=True))
        attention = (weights_raw / totals).astype(jnp.bfloat16)
        context = jnp.einsum('hqk,khd->qhd', attention.astype(jnp.float32), values.astype(jnp.float32)).astype(jnp.bfloat16)
        grouped = context.reshape(PACK, N_MP, HEADS * HS // N_MP).astype(jnp.float32)
        group_terms = jnp.einsum('rgk,gkd->rgd', grouped, out_groups).astype(jnp.bfloat16)
        group_terms = lax.optimization_barrier(group_terms).astype(jnp.float32)
        return lax.optimization_barrier(jnp.sum(group_terms, axis=1)).astype(jnp.bfloat16)
    attended = lax.map(one_pack, (packed.reshape(PACKS, PACK, D), image_ids)).reshape(TOKENS, D)
    return (packed, attended)
```

```python
import jax
import jax.numpy as jnp
from jax import lax
from jax.sharding import PartitionSpec as P

epsilon = 1e-06


def row_norm(values, scales):
    middle = jnp.mean(values, axis=-1, keepdims=True)
    spread = jnp.mean(values * values, axis=-1, keepdims=True) - middle * middle
    return (values - middle) * lax.rsqrt(spread + epsilon) * scales


def on_device(
    patches,
    send_start,
    run_length,
    slot_start,
    image_ids,
    norm_gain,
    qkv_weight,
    query_gain,
    key_gain,
    out_weight,
):
    pack_rows, feat_local = patches.shape
    pack_count = lax.axis_size("dp")
    mp_count = lax.axis_size("mp")
    capacity = 2 * pack_rows // pack_count
    local_cols = qkv_weight.shape[1] * qkv_weight.shape[2]
    offsets = jnp.arange(capacity, dtype=jnp.int32)
    rows = jnp.arange(pack_rows, dtype=jnp.int32)

    x = patches.astype(jnp.float32)
    sums = jnp.stack([jnp.sum(x, axis=-1), jnp.sum(x * x, axis=-1)])
    sums = lax.psum(sums, "mp") / (feat_local * mp_count)
    middle = sums[0][:, None]
    spread = sums[1][:, None] - middle * middle
    gain = lax.dynamic_slice_in_dim(norm_gain, lax.axis_index("mp") * feat_local, feat_local)
    normed = ((x - middle) * lax.rsqrt(spread + epsilon) * gain).astype(jnp.bfloat16)

    wide = lax.all_gather(normed, "mp", axis=1, tiled=True)
    slices = lax.all_to_all(wide, "dp", split_axis=1, concat_axis=0, tiled=True)

    tables = jnp.concatenate([send_start, run_length, slot_start], axis=0)[None]
    tables = lax.all_gather(tables, "dp", axis=0, tiled=True)
    starts, lengths, slots = tables[:, 0].T, tables[:, 1].T, tables[:, 2]
    inside = (rows >= slots[:, :, None]) & (rows < (slots + lengths)[:, :, None])
    base = jnp.arange(pack_count, dtype=jnp.int32)[None, :] * pack_rows + starts - slots
    origin = jnp.sum(jnp.where(inside, base[:, :, None] + rows, 0), axis=1).reshape(-1)
    chosen = (origin[:, None] == jnp.arange(origin.shape[0], dtype=jnp.int32)).astype(jnp.bfloat16)
    ordered = jnp.dot(chosen, slices, preferred_element_type=jnp.float32).astype(jnp.bfloat16)

    partial = jnp.dot(
        ordered, qkv_weight.reshape(qkv_weight.shape[0], local_cols), preferred_element_type=jnp.float32
    ).astype(jnp.bfloat16)
    projected = lax.psum_scatter(partial, "dp", scatter_dimension=0, tiled=True).astype(jnp.float32)

    own_rows = send_start[0][:, None] + offsets[None, :]
    occupied = offsets[None, :] < run_length[0][:, None]
    pick = (occupied[:, :, None] & (own_rows[:, :, None] == rows)).astype(jnp.bfloat16)
    outgoing = jnp.dot(
        pick.reshape(-1, pack_rows), patches, preferred_element_type=jnp.float32
    ).astype(jnp.bfloat16)
    arrived = lax.all_to_all(
        outgoing.reshape(pack_count, capacity, feat_local), "dp", split_axis=0, concat_axis=0, tiled=True
    )
    targets = (slot_start[0][:, None] + offsets[None, :]).reshape(-1)
    place = (rows[:, None] == targets[None, :]).astype(jnp.bfloat16)
    packed = jnp.dot(
        place, arrived.reshape(-1, feat_local), preferred_element_type=jnp.float32
    ).astype(jnp.bfloat16)

    head_size = query_gain.shape[0]
    heads_here = qkv_weight.shape[2] // head_size
    split_heads = projected.reshape(pack_rows, 3, heads_here, head_size)
    queries = row_norm(split_heads[:, 0], query_gain).astype(jnp.bfloat16)
    key_rows = row_norm(split_heads[:, 1], key_gain).astype(jnp.bfloat16)
    values = split_heads[:, 2].astype(jnp.bfloat16)
    scores = jnp.einsum(
        "qhd,khd->hqk", queries, key_rows, preferred_element_type=jnp.float32
    ) * head_size ** (-0.5)
    image_of = image_ids[0]
    same_image = image_of[:, None] == image_of[None, :]
    weights_raw = jnp.where(same_image[None], jnp.exp(scores), 0.0)
    totals = jnp.sum(weights_raw, axis=-1, keepdims=True)
    attention = (weights_raw / totals).astype(jnp.bfloat16)
    context = jnp.einsum(
        "hqk,khd->qhd", attention, values, preferred_element_type=jnp.float32
    ).astype(jnp.bfloat16)
    context = context.reshape(pack_rows, heads_here * head_size)
    partial_value = jnp.dot(context, out_weight, preferred_element_type=jnp.float32)
    attended = lax.psum_scatter(
        partial_value.astype(jnp.bfloat16), "mp", scatter_dimension=1, tiled=True
    )
    return (packed, attended)


def solution(mesh):
    return jax.shard_map(
        on_device,
        mesh=mesh,
        in_specs=(
            P("dp", "mp"),
            P("dp", None),
            P("dp", None),
            P("dp", None),
            P("dp", None),
            P(),
            P("dp", None, "mp"),
            P(),
            P(),
            P("mp", None),
        ),
        out_specs=(P("dp", "mp"), P("dp", "mp")),
        check_vma=False,
    )
```

```python
import functools

import jax
import jax.numpy as jnp
from jax import lax
from jax.experimental import pallas as pl
from jax.experimental.pallas import tpu as pltpu
from jax.sharding import PartitionSpec as P

epsilon = 1e-06


def row_norm(values, scales):
    middle = jnp.mean(values, axis=-1, keepdims=True)
    spread = jnp.mean(values * values, axis=-1, keepdims=True) - middle * middle
    return (values - middle) * lax.rsqrt(spread + epsilon) * scales


def plain_on_device(
    patches,
    send_start,
    run_length,
    slot_start,
    image_ids,
    norm_gain,
    qkv_weight,
    query_gain,
    key_gain,
    out_weight,
):
    pack_rows, feat_local = patches.shape
    pack_count = lax.axis_size("dp")
    mp_count = lax.axis_size("mp")
    capacity = 2 * pack_rows // pack_count
    local_cols = qkv_weight.shape[1] * qkv_weight.shape[2]
    offsets = jnp.arange(capacity, dtype=jnp.int32)
    rows = jnp.arange(pack_rows, dtype=jnp.int32)

    x = patches.astype(jnp.float32)
    sums = jnp.stack([jnp.sum(x, axis=-1), jnp.sum(x * x, axis=-1)])
    sums = lax.psum(sums, "mp") / (feat_local * mp_count)
    middle = sums[0][:, None]
    spread = sums[1][:, None] - middle * middle
    gain = lax.dynamic_slice_in_dim(norm_gain, lax.axis_index("mp") * feat_local, feat_local)
    normed = ((x - middle) * lax.rsqrt(spread + epsilon) * gain).astype(jnp.bfloat16)

    wide = lax.all_gather(normed, "mp", axis=1, tiled=True)
    slices = lax.all_to_all(wide, "dp", split_axis=1, concat_axis=0, tiled=True)

    tables = jnp.concatenate([send_start, run_length, slot_start], axis=0)[None]
    tables = lax.all_gather(tables, "dp", axis=0, tiled=True)
    starts, lengths, slots = tables[:, 0].T, tables[:, 1].T, tables[:, 2]
    inside = (rows >= slots[:, :, None]) & (rows < (slots + lengths)[:, :, None])
    base = jnp.arange(pack_count, dtype=jnp.int32)[None, :] * pack_rows + starts - slots
    origin = jnp.sum(jnp.where(inside, base[:, :, None] + rows, 0), axis=1).reshape(-1)
    chosen = (origin[:, None] == jnp.arange(origin.shape[0], dtype=jnp.int32)).astype(jnp.bfloat16)
    ordered = jnp.dot(chosen, slices, preferred_element_type=jnp.float32).astype(jnp.bfloat16)

    partial = jnp.dot(
        ordered, qkv_weight.reshape(qkv_weight.shape[0], local_cols), preferred_element_type=jnp.float32
    ).astype(jnp.bfloat16)
    projected = lax.psum_scatter(partial, "dp", scatter_dimension=0, tiled=True).astype(jnp.float32)

    own_rows = send_start[0][:, None] + offsets[None, :]
    occupied = offsets[None, :] < run_length[0][:, None]
    pick = (occupied[:, :, None] & (own_rows[:, :, None] == rows)).astype(jnp.bfloat16)
    outgoing = jnp.dot(
        pick.reshape(-1, pack_rows), patches, preferred_element_type=jnp.float32
    ).astype(jnp.bfloat16)
    arrived = lax.all_to_all(
        outgoing.reshape(pack_count, capacity, feat_local), "dp", split_axis=0, concat_axis=0, tiled=True
    )
    targets = (slot_start[0][:, None] + offsets[None, :]).reshape(-1)
    place = (rows[:, None] == targets[None, :]).astype(jnp.bfloat16)
    packed = jnp.dot(
        place, arrived.reshape(-1, feat_local), preferred_element_type=jnp.float32
    ).astype(jnp.bfloat16)

    head_size = query_gain.shape[0]
    heads_here = qkv_weight.shape[2] // head_size
    split_heads = projected.reshape(pack_rows, 3, heads_here, head_size)
    queries = row_norm(split_heads[:, 0], query_gain).astype(jnp.bfloat16)
    key_rows = row_norm(split_heads[:, 1], key_gain).astype(jnp.bfloat16)
    values = split_heads[:, 2].astype(jnp.bfloat16)
    scores = jnp.einsum(
        "qhd,khd->hqk", queries, key_rows, preferred_element_type=jnp.float32
    ) * head_size ** (-0.5)
    image_of = image_ids[0]
    same_image = image_of[:, None] == image_of[None, :]
    weights_raw = jnp.where(same_image[None], jnp.exp(scores), 0.0)
    totals = jnp.sum(weights_raw, axis=-1, keepdims=True)
    attention = (weights_raw / totals).astype(jnp.bfloat16)
    context = jnp.einsum(
        "hqk,khd->qhd", attention, values, preferred_element_type=jnp.float32
    ).astype(jnp.bfloat16)
    context = context.reshape(pack_rows, heads_here * head_size)
    partial_value = jnp.dot(context, out_weight, preferred_element_type=jnp.float32)
    attended = lax.psum_scatter(
        partial_value.astype(jnp.bfloat16), "mp", scatter_dimension=1, tiled=True
    )
    return (packed, attended)


MESH = pl.DeviceIdType.MESH
BF = jnp.bfloat16
F32 = jnp.float32


def fused_kernel(
    x_ref, ss_ref, rl_ref, sl_ref, ids_ref, ng_ref, qg_ref, kg_ref, w_hbm, ow_hbm,
    packed_ref, out_ref,
    w_ref, ow_ref, zbuf, nbuf, gbuf, outr, arr, tscr, tabs, perm, ordr,
    sbuf, rbuf, cbuf, crecv, qn, kn, vn, ctx, pbuf, zrecv,
    w_sem, zs, zr, asem, ar, rs, rr, ts, tr, ssem, sr, cs, cr, ps, pr,
):
    rows, feat = x_ref.shape
    n_dp, cap = outr.shape[0], outr.shape[1]
    kdim, cols = w_ref.shape[1], w_ref.shape[2]
    half = n_dp // 2 * rows
    d = lax.axis_index("dp")
    z = lax.axis_index("mp")
    k = d % 2
    cx = (d // 2) % 2
    cy = d // 4

    def peer_chip(oc):
        return ((cy + oc // 2) % 2) * 2 + (cx + oc % 2) % 2

    def peer(o):
        return peer_chip(o // 2) * 2 + (k + o % 2) % 2

    def remote(src, dst, s, r, dd, zz):
        return pltpu.make_async_remote_copy(
            src_ref=src, dst_ref=dst, send_sem=s, recv_sem=r,
            device_id=(dd, zz), device_id_type=MESH,
        )

    w_copy = pltpu.make_async_copy(w_hbm, w_ref, w_sem.at[0])
    ow_copy = pltpu.make_async_copy(ow_hbm, ow_ref, w_sem.at[1])
    w_copy.start()
    ow_copy.start()

    tscr[...] = jnp.zeros_like(tscr)
    tscr[0:1, 0:n_dp] = ss_ref[...]
    tscr[1:2, 0:n_dp] = rl_ref[...]
    tscr[2:3, 0:n_dp] = sl_ref[...]

    barrier = pltpu.get_barrier_semaphore()
    for o in range(1, 8):
        pl.semaphore_signal(barrier, inc=1, device_id=(peer(o), z), device_id_type=MESH)
    for o in range(1, 4):
        pl.semaphore_signal(barrier, inc=1, device_id=(d, (z + o) % 4), device_id_type=MESH)
    pl.semaphore_wait(barrier, 10)

    z_copies = [
        remote(x_ref, zbuf.at[z], zs.at[o - 1], zr.at[o - 1], d, (z + o) % 4)
        for o in (2, 1, 3)
    ]
    t_copies = [
        remote(tscr, tabs.at[d], ts.at[o - 1], tr.at[o - 1], peer(o), z) for o in range(1, 8)
    ]
    for copy in z_copies + t_copies:
        copy.start()
    zbuf[pl.ds(z, 1)] = x_ref[...][None]
    tabs[pl.ds(d, 1)] = tscr[...][None]

    ro = lax.broadcasted_iota(jnp.int32, (cap, rows), 0)
    rj = lax.broadcasted_iota(jnp.int32, (cap, rows), 1)
    for p in range(n_dp):
        start = tscr[0:1, p:p + 1]
        length = tscr[1:2, p:p + 1]
        pick = jnp.where((rj - ro == start) & (ro < length), 1.0, 0.0).astype(BF)
        outr[p] = jnp.dot(pick, x_ref[...], preferred_element_type=F32).astype(BF)
    r_copies = [
        remote(outr.at[peer(o)], arr.at[d], rs.at[o - 1], rr.at[o - 1], peer(o), z)
        for o in (6, 7, 2, 3, 4, 5, 1)
    ]
    for copy in r_copies:
        copy.start()
    arr[pl.ds(d, 1)] = outr[pl.ds(d, 1)]

    for copy in t_copies:
        copy.wait_recv()
    pi = lax.broadcasted_iota(jnp.int32, (rows, rows), 0)
    pj = lax.broadcasted_iota(jnp.int32, (rows, rows), 1)
    delta = pi - pj
    for p in range(n_dp):
        spot = pl.multiple_of((p // 2 + 4 * (1 - (p % 2 + k) % 2)) * rows, rows)
        for s in range(n_dp):
            start = tabs[s, 0:1, p:p + 1]
            length = tabs[s, 1:2, p:p + 1]
            slot = tabs[p, 2:3, s:s + 1]
            hit = (delta == slot - start) & (pj >= start) & (pj < start + length)
            perm[pl.ds(spot, rows), s * rows:(s + 1) * rows] = jnp.where(hit, 1.0, 0.0).astype(BF)

    for copy in z_copies:
        copy.wait_recv()

    step = 16
    total = float(feat * 4)

    def norm_rows(i, carry):
        span = pl.ds(pl.multiple_of(i * step, step), step)
        s1 = jnp.zeros((step, 1), F32)
        s2 = jnp.zeros((step, 1), F32)
        for b in range(4):
            v = zbuf[b, span, :].astype(F32)
            s1 += jnp.sum(v, axis=-1, keepdims=True)
            s2 += jnp.sum(v * v, axis=-1, keepdims=True)
        mid = s1 / total
        scale = lax.rsqrt(s2 / total - mid * mid + epsilon)
        for b in range(n_dp):
            lane = (b % 2) * kdim
            v = zbuf[b // 2, span, lane:lane + kdim].astype(F32)
            g = ng_ref[:, b * kdim:(b + 1) * kdim]
            nbuf[b, span, :] = ((v - mid) * scale * g).astype(BF)
        return carry

    lax.fori_loop(0, rows // step, norm_rows, 0)

    a_copies = [
        remote(nbuf.at[peer(o)], gbuf.at[d], asem.at[o - 1], ar.at[o - 1], peer(o), z)
        for o in (6, 7, 2, 3, 4, 5, 1)
    ]
    for copy in a_copies:
        copy.start()
    gbuf[pl.ds(d, 1)] = nbuf[pl.ds(d, 1)]

    for copy in r_copies:
        copy.wait_recv()
    si = lax.broadcasted_iota(jnp.int32, (rows, cap), 0)
    so = lax.broadcasted_iota(jnp.int32, (rows, cap), 1)
    place = jnp.concatenate(
        [
            jnp.where(si - so == tscr[2:3, s:s + 1], 1.0, 0.0)
            for s in range(n_dp)
        ],
        axis=1,
    ).astype(BF)
    packed_ref[...] = jnp.dot(
        place, arr[...].reshape(n_dp * cap, feat), preferred_element_type=F32
    ).astype(BF)

    for copy in a_copies:
        copy.wait_recv()
    w_copy.wait()

    tile = 256

    def order_half(h):
        def body(t, carry):
            lane = pl.ds(pl.multiple_of(t * tile, tile), tile)
            right = gbuf[:, :, lane].reshape(n_dp * rows, tile)
            ordr[:, lane] = jnp.dot(
                perm[h * half:(h + 1) * half, :], right, preferred_element_type=F32
            ).astype(BF)
            return carry

        lax.fori_loop(0, kdim // tile, body, 0)

    order_half(0)
    sibling = peer(1)
    s_copies = []
    for j in range(3):
        def body(t, carry, j=j):
            lane = pl.ds(pl.multiple_of(t * tile, tile), tile)
            sbuf[j, :, lane] = jnp.dot(
                ordr[...], w_ref[j, :, lane], preferred_element_type=F32
            ).astype(BF)
            return carry

        lax.fori_loop(0, cols // tile, body, 0)
        copy = remote(sbuf.at[j], rbuf.at[j], ssem.at[j], sr.at[j], sibling, z)
        copy.start()
        s_copies.append(copy)

    order_half(1)
    c_copies = [[], [], []]
    for j in range(3):
        s_copies[j].wait_recv()

        def body(t, carry, j=j):
            lane = pl.ds(pl.multiple_of(t * tile, tile), tile)
            got = jnp.dot(ordr[...], w_ref[j, :, lane], preferred_element_type=F32)
            got = (got + rbuf[j, :, lane].astype(F32)).astype(BF)
            cbuf[j, :, :, lane] = got.reshape(half // rows, rows, tile)
            return carry

        lax.fori_loop(0, cols // tile, body, 0)
        for oc in (3, 1, 2):
            copy = remote(
                cbuf.at[j, peer_chip(oc)], crecv.at[j, oc - 1],
                cs.at[j, oc - 1], cr.at[j, oc - 1], peer(2 * oc), z,
            )
            copy.start()
            c_copies[j].append(copy)

    hs = qg_ref.shape[1]
    heads = cols // hs
    chip = d // 2

    for j in range(3):
        for copy in c_copies[j]:
            copy.wait_recv()
        for h in range(heads):
            lane = slice(h * hs, (h + 1) * hs)
            v = cbuf[j, pl.ds(chip, 1), :, lane][0].astype(F32)
            for b in range(3):
                v += crecv[j, b, :, lane].astype(F32)
            if j < 2:
                mid = jnp.mean(v, axis=-1, keepdims=True)
                spread = jnp.mean(v * v, axis=-1, keepdims=True) - mid * mid
                gain = (qg_ref, kg_ref)[j][...]
                v = (v - mid) * lax.rsqrt(spread + epsilon) * gain
            (qn, kn, vn)[j][:, lane] = v.astype(BF)

    ids = jnp.broadcast_to(ids_ref[...], (rows, rows))
    same = ids == ids.T
    for h in range(heads):
        lane = slice(h * hs, (h + 1) * hs)
        scores = lax.dot_general(
            qn[:, lane], kn[:, lane], (((1,), (1,)), ((), ())), preferred_element_type=F32
        ) * hs ** (-0.5)
        raw = jnp.where(same, jnp.exp(scores), 0.0)
        att = (raw / jnp.sum(raw, axis=-1, keepdims=True)).astype(BF)
        ctx[:, lane] = jnp.dot(att, vn[:, lane], preferred_element_type=F32).astype(BF)

    ow_copy.wait()
    wide = 512
    p_copies = []
    for i, o in enumerate((2, 1, 3, 0)):
        goal = (z + o) % 4

        def body(t, carry, i=i, goal=goal):
            lane = pl.ds(pl.multiple_of(t * wide, wide), wide)
            from_lane = pl.ds(pl.multiple_of(goal * feat + t * wide, wide), wide)
            pbuf[i, :, lane] = jnp.dot(
                ctx[...], ow_ref[:, from_lane], preferred_element_type=F32
            ).astype(BF)
            return carry

        lax.fori_loop(0, feat // wide, body, 0)
        if o:
            copy = remote(pbuf.at[i], zrecv.at[i], ps.at[i], pr.at[i], d, goal)
            copy.start()
            p_copies.append(copy)
    for copy in p_copies:
        copy.wait_recv()
    result = pbuf[3].astype(F32)
    for i in range(3):
        result += zrecv[i].astype(F32)
    out_ref[...] = result.astype(BF)

    for copy in z_copies + t_copies + r_copies + a_copies + s_copies + sum(c_copies, []) + p_copies:
        copy.wait_send()


def fused_on_device(
    patches,
    send_start,
    run_length,
    slot_start,
    image_ids,
    norm_gain,
    qkv_weight,
    query_gain,
    key_gain,
    out_weight,
):
    rows, feat = patches.shape
    n_dp = lax.axis_size("dp")
    n_mp = lax.axis_size("mp")
    cap = 2 * rows // n_dp
    kdim, _, cols = qkv_weight.shape
    width = out_weight.shape[1]
    half = n_dp // 2 * rows
    weight = jnp.transpose(qkv_weight, (1, 0, 2))
    vm = pl.BlockSpec(memory_space=pltpu.VMEM)
    hbm = pl.BlockSpec(memory_space=pl.ANY)
    dma = pltpu.SemaphoreType.DMA
    return pl.pallas_call(
        fused_kernel,
        out_shape=(
            jax.ShapeDtypeStruct((rows, feat), BF),
            jax.ShapeDtypeStruct((rows, feat), BF),
        ),
        in_specs=[vm] * 8 + [hbm] * 2,
        out_specs=(vm, vm),
        scratch_shapes=[
            pltpu.VMEM((3, kdim, cols), BF),
            pltpu.VMEM((cols, width), BF),
            pltpu.VMEM((n_mp, rows, feat), BF),
            pltpu.VMEM((n_dp, rows, kdim), BF),
            pltpu.VMEM((n_dp, rows, kdim), BF),
            pltpu.VMEM((n_dp, cap, feat), BF),
            pltpu.VMEM((n_dp, cap, feat), BF),
            pltpu.VMEM((8, 128), jnp.int32),
            pltpu.VMEM((n_dp, 8, 128), jnp.int32),
            pltpu.VMEM((2 * half, 2 * half), BF),
            pltpu.VMEM((half, kdim), BF),
            pltpu.VMEM((3, half, cols), BF),
            pltpu.VMEM((3, half, cols), BF),
            pltpu.VMEM((3, n_dp // 2, rows, cols), BF),
            pltpu.VMEM((3, n_dp // 2 - 1, rows, cols), BF),
            pltpu.VMEM((rows, cols), BF),
            pltpu.VMEM((rows, cols), BF),
            pltpu.VMEM((rows, cols), BF),
            pltpu.VMEM((rows, cols), BF),
            pltpu.VMEM((n_mp, rows, feat), BF),
            pltpu.VMEM((n_mp - 1, rows, feat), BF),
            dma((2,)),
            dma((3,)), dma((3,)),
            dma((7,)), dma((7,)),
            dma((7,)), dma((7,)),
            dma((7,)), dma((7,)),
            dma((3,)), dma((3,)),
            dma((3, 3)), dma((3, 3)),
            dma((3,)), dma((3,)),
        ],
        compiler_params=pltpu.CompilerParams(
            collective_id=0, has_side_effects=True, vmem_limit_bytes=60 * 1024 * 1024
        ),
    )(
        patches, send_start, run_length, slot_start, image_ids,
        norm_gain.reshape(1, -1), query_gain.reshape(1, -1), key_gain.reshape(1, -1),
        weight, out_weight,
    )


def solution(mesh):
    small = mesh.shape["dp"] == 8 and mesh.shape["mp"] == 4
    return jax.shard_map(
        fused_on_device if small else plain_on_device,
        mesh=mesh,
        in_specs=(
            P("dp", "mp"),
            P("dp", None),
            P("dp", None),
            P("dp", None),
            P("dp", None),
            P(),
            P("dp", None, "mp"),
            P(),
            P(),
            P("mp", None),
        ),
        out_specs=(P("dp", "mp"), P("dp", "mp")),
        check_vma=False,
    )
```

```python
import functools

import jax
import jax.numpy as jnp
from jax import lax
from jax.experimental import pallas as pl
from jax.experimental.pallas import tpu as pltpu
from jax.sharding import PartitionSpec as P

epsilon = 1e-06


def row_norm(values, scales):
    middle = jnp.mean(values, axis=-1, keepdims=True)
    spread = jnp.mean(values * values, axis=-1, keepdims=True) - middle * middle
    return (values - middle) * lax.rsqrt(spread + epsilon) * scales


def plain_on_device(
    patches,
    send_start,
    run_length,
    slot_start,
    image_ids,
    norm_gain,
    qkv_weight,
    query_gain,
    key_gain,
    out_weight,
):
    pack_rows, feat_local = patches.shape
    pack_count = lax.axis_size("dp")
    mp_count = lax.axis_size("mp")
    capacity = 2 * pack_rows // pack_count
    local_cols = qkv_weight.shape[1] * qkv_weight.shape[2]
    offsets = jnp.arange(capacity, dtype=jnp.int32)
    rows = jnp.arange(pack_rows, dtype=jnp.int32)

    x = patches.astype(jnp.float32)
    sums = jnp.stack([jnp.sum(x, axis=-1), jnp.sum(x * x, axis=-1)])
    sums = lax.psum(sums, "mp") / (feat_local * mp_count)
    middle = sums[0][:, None]
    spread = sums[1][:, None] - middle * middle
    gain = lax.dynamic_slice_in_dim(norm_gain, lax.axis_index("mp") * feat_local, feat_local)
    normed = ((x - middle) * lax.rsqrt(spread + epsilon) * gain).astype(jnp.bfloat16)

    wide = lax.all_gather(normed, "mp", axis=1, tiled=True)
    slices = lax.all_to_all(wide, "dp", split_axis=1, concat_axis=0, tiled=True)

    tables = jnp.concatenate([send_start, run_length, slot_start], axis=0)[None]
    tables = lax.all_gather(tables, "dp", axis=0, tiled=True)
    starts, lengths, slots = tables[:, 0].T, tables[:, 1].T, tables[:, 2]
    inside = (rows >= slots[:, :, None]) & (rows < (slots + lengths)[:, :, None])
    base = jnp.arange(pack_count, dtype=jnp.int32)[None, :] * pack_rows + starts - slots
    origin = jnp.sum(jnp.where(inside, base[:, :, None] + rows, 0), axis=1).reshape(-1)
    chosen = (origin[:, None] == jnp.arange(origin.shape[0], dtype=jnp.int32)).astype(jnp.bfloat16)
    ordered = jnp.dot(chosen, slices, preferred_element_type=jnp.float32).astype(jnp.bfloat16)

    partial = jnp.dot(
        ordered, qkv_weight.reshape(qkv_weight.shape[0], local_cols), preferred_element_type=jnp.float32
    ).astype(jnp.bfloat16)
    projected = lax.psum_scatter(partial, "dp", scatter_dimension=0, tiled=True).astype(jnp.float32)

    own_rows = send_start[0][:, None] + offsets[None, :]
    occupied = offsets[None, :] < run_length[0][:, None]
    pick = (occupied[:, :, None] & (own_rows[:, :, None] == rows)).astype(jnp.bfloat16)
    outgoing = jnp.dot(
        pick.reshape(-1, pack_rows), patches, preferred_element_type=jnp.float32
    ).astype(jnp.bfloat16)
    arrived = lax.all_to_all(
        outgoing.reshape(pack_count, capacity, feat_local), "dp", split_axis=0, concat_axis=0, tiled=True
    )
    targets = (slot_start[0][:, None] + offsets[None, :]).reshape(-1)
    place = (rows[:, None] == targets[None, :]).astype(jnp.bfloat16)
    packed = jnp.dot(
        place, arrived.reshape(-1, feat_local), preferred_element_type=jnp.float32
    ).astype(jnp.bfloat16)

    head_size = query_gain.shape[0]
    heads_here = qkv_weight.shape[2] // head_size
    split_heads = projected.reshape(pack_rows, 3, heads_here, head_size)
    queries = row_norm(split_heads[:, 0], query_gain).astype(jnp.bfloat16)
    key_rows = row_norm(split_heads[:, 1], key_gain).astype(jnp.bfloat16)
    values = split_heads[:, 2].astype(jnp.bfloat16)
    scores = jnp.einsum(
        "qhd,khd->hqk", queries, key_rows, preferred_element_type=jnp.float32
    ) * head_size ** (-0.5)
    image_of = image_ids[0]
    same_image = image_of[:, None] == image_of[None, :]
    weights_raw = jnp.where(same_image[None], jnp.exp(scores), 0.0)
    totals = jnp.sum(weights_raw, axis=-1, keepdims=True)
    attention = (weights_raw / totals).astype(jnp.bfloat16)
    context = jnp.einsum(
        "hqk,khd->qhd", attention, values, preferred_element_type=jnp.float32
    ).astype(jnp.bfloat16)
    context = context.reshape(pack_rows, heads_here * head_size)
    partial_value = jnp.dot(context, out_weight, preferred_element_type=jnp.float32)
    attended = lax.psum_scatter(
        partial_value.astype(jnp.bfloat16), "mp", scatter_dimension=1, tiled=True
    )
    return (packed, attended)


MESH = pl.DeviceIdType.MESH
BF = jnp.bfloat16
F32 = jnp.float32


def fused_kernel(
    x_ref, ss_ref, rl_ref, sl_ref, ids_ref, ng_ref, qg_ref, kg_ref, w_hbm, ow_hbm,
    packed_ref, out_ref,
    w_ref, ow_ref, zbuf, nbuf, gbuf, outr, arr, tscr, tabs, perm, ordr,
    sbuf, rbuf, cbuf, crecv, qn, kn, vn, ctx, pbuf, psend, zrecv,
    w_sem, zs, zr, asem, ar, rs, rr, ts, tr, ssem, sr, cs, cr, ps, pr,
):
    rows, feat = x_ref.shape
    n_dp, cap = outr.shape[0], outr.shape[1]
    kdim, cols = w_ref.shape[1], w_ref.shape[2]
    half = n_dp // 2 * rows
    d = lax.axis_index("dp")
    z = lax.axis_index("mp")
    k = d % 2
    cx = (d // 2) % 2
    cy = d // 4

    def peer_chip(oc):
        return ((cy + oc // 2) % 2) * 2 + (cx + oc % 2) % 2

    def peer(o):
        return peer_chip(o // 2) * 2 + (k + o % 2) % 2

    def remote(src, dst, s, r, dd, zz):
        return pltpu.make_async_remote_copy(
            src_ref=src, dst_ref=dst, send_sem=s, recv_sem=r,
            device_id=(dd, zz), device_id_type=MESH,
        )

    w_copy = pltpu.make_async_copy(w_hbm, w_ref, w_sem.at[0])
    ow_copy = pltpu.make_async_copy(ow_hbm, ow_ref, w_sem.at[1])
    w_copy.start()
    ow_copy.start()

    tscr[...] = jnp.zeros_like(tscr)
    tscr[0:1, 0:n_dp] = ss_ref[...]
    tscr[1:2, 0:n_dp] = rl_ref[...]
    tscr[2:3, 0:n_dp] = sl_ref[...]

    barrier = pltpu.get_barrier_semaphore()
    for o in range(1, 8):
        pl.semaphore_signal(barrier, inc=1, device_id=(peer(o), z), device_id_type=MESH)
    for way in range(2):
        @pl.when(z < 3 if way == 0 else z > 0)
        def _(way=way):
            pl.semaphore_signal(
                barrier, inc=1, device_id=(d, z + 1 - 2 * way), device_id_type=MESH
            )
    near = jnp.where((z == 0) | (z == 3), 1, 2)
    pl.semaphore_wait(barrier, 7 + near)

    hrows = rows // 2

    def z_copy(block, h, way):
        span = slice(h * hrows, (h + 1) * hrows)
        return remote(
            zbuf.at[block, span], zbuf.at[block, span],
            zs.at[way, h, block], zr.at[h, block], d, z + 1 - 2 * way,
        )

    def z_send(h, way):
        @pl.when(z < 3 if way == 0 else z > 0)
        def _():
            z_copy(z, h, way).start()

    def z_pass(h):
        for t in range(1, 4):
            for way in range(2):
                block = z - t if way == 0 else z + t

                @pl.when(block >= 0 if way == 0 else block <= 3)
                def _(block=block, way=way):
                    z_copy(block, h, way).wait_recv()

                    @pl.when(z < 3 if way == 0 else z > 0)
                    def _():
                        z_copy(block, h, way).start()

                if h == 0:
                    @pl.when(z == t if way == 0 else z == 3 - t)
                    def _(way=way):
                        z_send(1, way)

    def z_drain():
        for h in range(2):
            for t in range(4):
                for way in range(2):
                    block = z - t if way == 0 else z + t

                    @pl.when((block >= 0) & (z < 3) if way == 0 else (block <= 3) & (z > 0))
                    def _(block=block, way=way, h=h):
                        z_copy(block, h, way).wait_send()

    zbuf[pl.ds(z, 1)] = x_ref[...][None]
    for way in range(2):
        z_send(0, way)
        @pl.when(z == 0 if way == 0 else z == 3)
        def _(way=way):
            z_send(1, way)

    t_copies = [
        remote(tscr, tabs.at[d], ts.at[o - 1], tr.at[o - 1], peer(o), z) for o in range(1, 8)
    ]
    for copy in t_copies:
        copy.start()
    tabs[pl.ds(d, 1)] = tscr[...][None]

    ro = lax.broadcasted_iota(jnp.int32, (cap, rows), 0)
    rj = lax.broadcasted_iota(jnp.int32, (cap, rows), 1)
    for p in range(n_dp):
        start = tscr[0:1, p:p + 1]
        length = tscr[1:2, p:p + 1]
        pick = jnp.where((rj - ro == start) & (ro < length), 1.0, 0.0).astype(BF)
        outr[p] = jnp.dot(pick, x_ref[...], preferred_element_type=F32).astype(BF)
    r_copies = [
        remote(outr.at[peer(o)], arr.at[d], rs.at[o - 1], rr.at[o - 1], peer(o), z)
        for o in (6, 7, 2, 3, 4, 5, 1)
    ]
    for copy in r_copies:
        copy.start()
    arr[pl.ds(d, 1)] = outr[pl.ds(d, 1)]

    step = 16
    total = float(feat * 4)

    def norm_rows(i, carry):
        span = pl.ds(pl.multiple_of(i * step, step), step)
        s1 = jnp.zeros((step, 1), F32)
        s2 = jnp.zeros((step, 1), F32)
        for b in range(4):
            v = zbuf[b, span, :].astype(F32)
            s1 += jnp.sum(v, axis=-1, keepdims=True)
            s2 += jnp.sum(v * v, axis=-1, keepdims=True)
        mid = s1 / total
        scale = lax.rsqrt(s2 / total - mid * mid + epsilon)
        for b in range(n_dp):
            lane = (b % 2) * kdim
            v = zbuf[b // 2, span, lane:lane + kdim].astype(F32)
            g = ng_ref[:, b * kdim:(b + 1) * kdim]
            nbuf[b, span, :] = ((v - mid) * scale * g).astype(BF)
        return carry

    a_copies = []
    for h in range(2):
        span = slice(h * hrows, (h + 1) * hrows)
        z_pass(h)
        lax.fori_loop(h * (hrows // step), (h + 1) * (hrows // step), norm_rows, 0)
        for o in (6, 7, 2, 3, 4, 5, 1):
            copy = remote(
                nbuf.at[peer(o), span], gbuf.at[d, span],
                asem.at[h, o - 1], ar.at[h, o - 1], peer(o), z,
            )
            copy.start()
            a_copies.append(copy)
    gbuf[pl.ds(d, 1)] = nbuf[pl.ds(d, 1)]

    for copy in t_copies:
        copy.wait_recv()
    pi = lax.broadcasted_iota(jnp.int32, (rows, rows), 0)
    pj = lax.broadcasted_iota(jnp.int32, (rows, rows), 1)
    delta = pi - pj
    for p in range(n_dp):
        spot = pl.multiple_of((p // 2 + 4 * (1 - (p % 2 + k) % 2)) * rows, rows)
        for s in range(n_dp):
            start = tabs[s, 0:1, p:p + 1]
            length = tabs[s, 1:2, p:p + 1]
            slot = tabs[p, 2:3, s:s + 1]
            hit = (delta == slot - start) & (pj >= start) & (pj < start + length)
            perm[pl.ds(spot, rows), s * rows:(s + 1) * rows] = jnp.where(hit, 1.0, 0.0).astype(BF)

    for copy in r_copies:
        copy.wait_recv()
    si = lax.broadcasted_iota(jnp.int32, (rows, cap), 0)
    so = lax.broadcasted_iota(jnp.int32, (rows, cap), 1)
    place = jnp.concatenate(
        [
            jnp.where(si - so == tscr[2:3, s:s + 1], 1.0, 0.0)
            for s in range(n_dp)
        ],
        axis=1,
    ).astype(BF)
    packed_ref[...] = jnp.dot(
        place, arr[...].reshape(n_dp * cap, feat), preferred_element_type=F32
    ).astype(BF)

    for copy in a_copies:
        copy.wait_recv()
    w_copy.wait()

    tile = 256

    def order_half(h):
        span = slice(h * half, (h + 1) * half)

        def body(t, carry):
            lane = pl.ds(pl.multiple_of(t * tile, tile), tile)
            right = gbuf[:, :, lane].reshape(n_dp * rows, tile)
            ordr[span, lane] = jnp.dot(
                perm[span, :], right, preferred_element_type=F32
            ).astype(BF)
            return carry

        lax.fori_loop(0, kdim // tile, body, 0)

    sibling = peer(1)
    s_copies = []
    c_copies = [[], [], []]

    def sibling_part(j):
        def body(t, carry):
            lane = pl.ds(pl.multiple_of(t * tile, tile), tile)
            sbuf[j, :, lane] = jnp.dot(
                ordr[:half, :], w_ref[j, :, lane], preferred_element_type=F32
            ).astype(BF)
            return carry

        lax.fori_loop(0, cols // tile, body, 0)
        copy = remote(sbuf.at[j], rbuf.at[j], ssem.at[j], sr.at[j], sibling, z)
        copy.start()
        s_copies.append(copy)

    def own_part(j):
        s_copies[j].wait_recv()

        def body(t, carry):
            lane = pl.ds(pl.multiple_of(t * tile, tile), tile)
            got = jnp.dot(ordr[half:, :], w_ref[j, :, lane], preferred_element_type=F32)
            got = (got + rbuf[j, :, lane].astype(F32)).astype(BF)
            cbuf[j, :, :, lane] = got.reshape(half // rows, rows, tile)
            return carry

        lax.fori_loop(0, cols // tile, body, 0)
        for oc in (3, 1, 2):
            copy = remote(
                cbuf.at[j, peer_chip(oc)], crecv.at[j, oc - 1],
                cs.at[j, oc - 1], cr.at[j, oc - 1], peer(2 * oc), z,
            )
            copy.start()
            c_copies[j].append(copy)

    order_half(0)
    sibling_part(0)
    order_half(1)
    sibling_part(1)
    own_part(0)
    sibling_part(2)
    own_part(1)
    own_part(2)

    hs = qg_ref.shape[1]
    heads = cols // hs
    chip = d // 2

    for j in range(3):
        for copy in c_copies[j]:
            copy.wait_recv()
        for h in range(heads):
            lane = slice(h * hs, (h + 1) * hs)
            v = cbuf[j, pl.ds(chip, 1), :, lane][0].astype(F32)
            for b in range(3):
                v += crecv[j, b, :, lane].astype(F32)
            if j < 2:
                mid = jnp.mean(v, axis=-1, keepdims=True)
                spread = jnp.mean(v * v, axis=-1, keepdims=True) - mid * mid
                gain = (qg_ref, kg_ref)[j][...]
                v = (v - mid) * lax.rsqrt(spread + epsilon) * gain
            (qn, kn, vn)[j][:, lane] = v.astype(BF)

    ids = jnp.broadcast_to(ids_ref[...], (rows, rows))
    same = ids == ids.T
    for h in range(heads):
        lane = slice(h * hs, (h + 1) * hs)
        scores = lax.dot_general(
            qn[:, lane], kn[:, lane], (((1,), (1,)), ((), ())), preferred_element_type=F32
        ) * hs ** (-0.5)
        raw = jnp.where(same, jnp.exp(scores), 0.0)
        att = (raw / jnp.sum(raw, axis=-1, keepdims=True)).astype(BF)
        ctx[:, lane] = jnp.dot(att, vn[:, lane], preferred_element_type=F32).astype(BF)

    ow_copy.wait()
    wide = 512

    def p_copy(m, way):
        return remote(
            psend.at[m], zrecv.at[way, m], ps.at[m], pr.at[way, m], d, z + 1 - 2 * way
        )

    for m in (3, 0, 2, 1):
        def body(t, carry, m=m):
            lane = pl.ds(pl.multiple_of(t * wide, wide), wide)
            from_lane = pl.ds(pl.multiple_of(m * feat + t * wide, wide), wide)
            got = jnp.dot(ctx[...], ow_ref[:, from_lane], preferred_element_type=F32)
            pbuf[m, :, lane] = got.astype(BF)
            return carry

        lax.fori_loop(0, feat // wide, body, 0)

        for way, end in ((0, 0), (1, 3)):
            if m != end:
                @pl.when(z == end)
                def _(m=m, way=way):
                    psend[m] = pbuf[m]
                    p_copy(m, way).start()

    for at, m in ((1, 3), (2, 0), (1, 2), (2, 1), (2, 3), (1, 0)):
        way = 0 if m > at else 1

        @pl.when(z == at)
        def _(m=m, way=way):
            p_copy(m, way).wait_recv()
            psend[m] = (pbuf[m].astype(F32) + zrecv[way, m].astype(F32)).astype(BF)
            p_copy(m, way).start()

    for way, end in ((0, 0), (1, 3)):
        @pl.when(z != end)
        def _(way=way):
            p_copy(z, way).wait_recv()

    mine = pbuf[pl.ds(z, 1)][0].astype(F32)

    @pl.when(z == 0)
    def _():
        out_ref[...] = (mine + zrecv[1, 0].astype(F32)).astype(BF)

    @pl.when(z == 3)
    def _():
        out_ref[...] = (mine + zrecv[0, 3].astype(F32)).astype(BF)

    for at in (1, 2):
        @pl.when(z == at)
        def _(at=at):
            both = zrecv[0, at].astype(F32) + zrecv[1, at].astype(F32)
            out_ref[...] = (mine + both).astype(BF)

    for m in range(4):
        @pl.when(z < m)
        def _(m=m):
            p_copy(m, 0).wait_send()

        @pl.when(z > m)
        def _(m=m):
            p_copy(m, 1).wait_send()

    for copy in t_copies + r_copies + a_copies + s_copies + sum(c_copies, []):
        copy.wait_send()
    z_drain()


def fused_on_device(
    patches,
    send_start,
    run_length,
    slot_start,
    image_ids,
    norm_gain,
    qkv_weight,
    query_gain,
    key_gain,
    out_weight,
):
    rows, feat = patches.shape
    n_dp = lax.axis_size("dp")
    n_mp = lax.axis_size("mp")
    cap = 2 * rows // n_dp
    kdim, _, cols = qkv_weight.shape
    width = out_weight.shape[1]
    half = n_dp // 2 * rows
    weight = jnp.transpose(qkv_weight, (1, 0, 2))
    vm = pl.BlockSpec(memory_space=pltpu.VMEM)
    hbm = pl.BlockSpec(memory_space=pl.ANY)
    dma = pltpu.SemaphoreType.DMA
    return pl.pallas_call(
        fused_kernel,
        out_shape=(
            jax.ShapeDtypeStruct((rows, feat), BF),
            jax.ShapeDtypeStruct((rows, feat), BF),
        ),
        in_specs=[vm] * 8 + [hbm] * 2,
        out_specs=(vm, vm),
        scratch_shapes=[
            pltpu.VMEM((3, kdim, cols), BF),
            pltpu.VMEM((cols, width), BF),
            pltpu.VMEM((n_mp, rows, feat), BF),
            pltpu.VMEM((n_dp, rows, kdim), BF),
            pltpu.VMEM((n_dp, rows, kdim), BF),
            pltpu.VMEM((n_dp, cap, feat), BF),
            pltpu.VMEM((n_dp, cap, feat), BF),
            pltpu.VMEM((8, 128), jnp.int32),
            pltpu.VMEM((n_dp, 8, 128), jnp.int32),
            pltpu.VMEM((2 * half, 2 * half), BF),
            pltpu.VMEM((2 * half, kdim), BF),
            pltpu.VMEM((3, half, cols), BF),
            pltpu.VMEM((3, half, cols), BF),
            pltpu.VMEM((3, n_dp // 2, rows, cols), BF),
            pltpu.VMEM((3, n_dp // 2 - 1, rows, cols), BF),
            pltpu.VMEM((rows, cols), BF),
            pltpu.VMEM((rows, cols), BF),
            pltpu.VMEM((rows, cols), BF),
            pltpu.VMEM((rows, cols), BF),
            pltpu.VMEM((n_mp, rows, feat), BF),
            pltpu.VMEM((n_mp, rows, feat), BF),
            pltpu.VMEM((2, n_mp, rows, feat), BF),
            dma((2,)),
            dma((2, 2, n_mp)), dma((2, n_mp)),
            dma((2, 7)), dma((2, 7)),
            dma((7,)), dma((7,)),
            dma((7,)), dma((7,)),
            dma((3,)), dma((3,)),
            dma((3, 3)), dma((3, 3)),
            dma((n_mp,)), dma((2, n_mp)),
        ],
        compiler_params=pltpu.CompilerParams(
            collective_id=0, has_side_effects=True, vmem_limit_bytes=60 * 1024 * 1024
        ),
    )(
        patches, send_start, run_length, slot_start, image_ids,
        norm_gain.reshape(1, -1), query_gain.reshape(1, -1), key_gain.reshape(1, -1),
        weight, out_weight,
    )


def solution(mesh):
    small = mesh.shape["dp"] == 8 and mesh.shape["mp"] == 4
    return jax.shard_map(
        fused_on_device if small else plain_on_device,
        mesh=mesh,
        in_specs=(
            P("dp", "mp"),
            P("dp", None),
            P("dp", None),
            P("dp", None),
            P("dp", None),
            P(),
            P("dp", None, "mp"),
            P(),
            P(),
            P("mp", None),
        ),
        out_specs=(P("dp", "mp"), P("dp", "mp")),
        check_vma=False,
    )
```

```python
import functools

import jax
import jax.numpy as jnp
from jax import lax
from jax.experimental import pallas as pl
from jax.experimental.pallas import tpu as pltpu
from jax.sharding import PartitionSpec as P

epsilon = 1e-06


def row_norm(values, scales):
    middle = jnp.mean(values, axis=-1, keepdims=True)
    spread = jnp.mean(values * values, axis=-1, keepdims=True) - middle * middle
    return (values - middle) * lax.rsqrt(spread + epsilon) * scales


def plain_on_device(
    patches,
    send_start,
    run_length,
    slot_start,
    image_ids,
    norm_gain,
    qkv_weight,
    query_gain,
    key_gain,
    out_weight,
):
    pack_rows, feat_local = patches.shape
    pack_count = lax.axis_size("dp")
    mp_count = lax.axis_size("mp")
    capacity = 2 * pack_rows // pack_count
    local_cols = qkv_weight.shape[1] * qkv_weight.shape[2]
    offsets = jnp.arange(capacity, dtype=jnp.int32)
    rows = jnp.arange(pack_rows, dtype=jnp.int32)

    x = patches.astype(jnp.float32)
    sums = jnp.stack([jnp.sum(x, axis=-1), jnp.sum(x * x, axis=-1)])
    sums = lax.psum(sums, "mp") / (feat_local * mp_count)
    middle = sums[0][:, None]
    spread = sums[1][:, None] - middle * middle
    gain = lax.dynamic_slice_in_dim(norm_gain, lax.axis_index("mp") * feat_local, feat_local)
    normed = ((x - middle) * lax.rsqrt(spread + epsilon) * gain).astype(jnp.bfloat16)

    wide = lax.all_gather(normed, "mp", axis=1, tiled=True)
    slices = lax.all_to_all(wide, "dp", split_axis=1, concat_axis=0, tiled=True)

    tables = jnp.concatenate([send_start, run_length, slot_start], axis=0)[None]
    tables = lax.all_gather(tables, "dp", axis=0, tiled=True)
    starts, lengths, slots = tables[:, 0].T, tables[:, 1].T, tables[:, 2]
    inside = (rows >= slots[:, :, None]) & (rows < (slots + lengths)[:, :, None])
    base = jnp.arange(pack_count, dtype=jnp.int32)[None, :] * pack_rows + starts - slots
    origin = jnp.sum(jnp.where(inside, base[:, :, None] + rows, 0), axis=1).reshape(-1)
    chosen = (origin[:, None] == jnp.arange(origin.shape[0], dtype=jnp.int32)).astype(jnp.bfloat16)
    ordered = jnp.dot(chosen, slices, preferred_element_type=jnp.float32).astype(jnp.bfloat16)

    partial = jnp.dot(
        ordered, qkv_weight.reshape(qkv_weight.shape[0], local_cols), preferred_element_type=jnp.float32
    ).astype(jnp.bfloat16)
    projected = lax.psum_scatter(partial, "dp", scatter_dimension=0, tiled=True).astype(jnp.float32)

    own_rows = send_start[0][:, None] + offsets[None, :]
    occupied = offsets[None, :] < run_length[0][:, None]
    pick = (occupied[:, :, None] & (own_rows[:, :, None] == rows)).astype(jnp.bfloat16)
    outgoing = jnp.dot(
        pick.reshape(-1, pack_rows), patches, preferred_element_type=jnp.float32
    ).astype(jnp.bfloat16)
    arrived = lax.all_to_all(
        outgoing.reshape(pack_count, capacity, feat_local), "dp", split_axis=0, concat_axis=0, tiled=True
    )
    targets = (slot_start[0][:, None] + offsets[None, :]).reshape(-1)
    place = (rows[:, None] == targets[None, :]).astype(jnp.bfloat16)
    packed = jnp.dot(
        place, arrived.reshape(-1, feat_local), preferred_element_type=jnp.float32
    ).astype(jnp.bfloat16)

    head_size = query_gain.shape[0]
    heads_here = qkv_weight.shape[2] // head_size
    split_heads = projected.reshape(pack_rows, 3, heads_here, head_size)
    queries = row_norm(split_heads[:, 0], query_gain).astype(jnp.bfloat16)
    key_rows = row_norm(split_heads[:, 1], key_gain).astype(jnp.bfloat16)
    values = split_heads[:, 2].astype(jnp.bfloat16)
    scores = jnp.einsum(
        "qhd,khd->hqk", queries, key_rows, preferred_element_type=jnp.float32
    ) * head_size ** (-0.5)
    image_of = image_ids[0]
    same_image = image_of[:, None] == image_of[None, :]
    weights_raw = jnp.where(same_image[None], jnp.exp(scores), 0.0)
    totals = jnp.sum(weights_raw, axis=-1, keepdims=True)
    attention = (weights_raw / totals).astype(jnp.bfloat16)
    context = jnp.einsum(
        "hqk,khd->qhd", attention, values, preferred_element_type=jnp.float32
    ).astype(jnp.bfloat16)
    context = context.reshape(pack_rows, heads_here * head_size)
    partial_value = jnp.dot(context, out_weight, preferred_element_type=jnp.float32)
    attended = lax.psum_scatter(
        partial_value.astype(jnp.bfloat16), "mp", scatter_dimension=1, tiled=True
    )
    return (packed, attended)


MESH = pl.DeviceIdType.MESH
BF = jnp.bfloat16
F32 = jnp.float32


def fused_kernel(
    x_ref, ss_ref, rl_ref, sl_ref, ids_ref, ng_ref, qg_ref, kg_ref, w_hbm, ow_hbm,
    packed_ref, out_ref,
    w_ref, ow_ref, zbuf, nbuf, gbuf, outr, arr, tscr, tabs, perm, ordr,
    sbuf, rbuf, cbuf, crecv, qn, kn, vn, ctx, pbuf, psend, zrecv,
    w_sem, zs, zr, asem, ar, rs, rr, ts, tr, ssem, sr, cs, cr, ps, pr,
):
    rows, feat = x_ref.shape
    n_dp, cap = outr.shape[0], outr.shape[1]
    kdim, cols = w_ref.shape[1], w_ref.shape[2]
    half = n_dp // 2 * rows
    d = lax.axis_index("dp")
    z = lax.axis_index("mp")
    k = d % 2
    cx = (d // 2) % 2
    cy = d // 4

    def peer_chip(oc):
        return ((cy + oc // 2) % 2) * 2 + (cx + oc % 2) % 2

    def peer(o):
        return peer_chip(o // 2) * 2 + (k + o % 2) % 2

    def remote(src, dst, s, r, dd, zz):
        return pltpu.make_async_remote_copy(
            src_ref=src, dst_ref=dst, send_sem=s, recv_sem=r,
            device_id=(dd, zz), device_id_type=MESH,
        )

    w_copy = pltpu.make_async_copy(w_hbm, w_ref, w_sem.at[0])
    ow_copy = pltpu.make_async_copy(ow_hbm, ow_ref, w_sem.at[1])
    w_copy.start()
    ow_copy.start()

    tscr[...] = jnp.zeros_like(tscr)
    tscr[0:1, 0:n_dp] = ss_ref[...]
    tscr[1:2, 0:n_dp] = rl_ref[...]
    tscr[2:3, 0:n_dp] = sl_ref[...]

    barrier = pltpu.get_barrier_semaphore()
    for o in range(1, 8):
        pl.semaphore_signal(barrier, inc=1, device_id=(peer(o), z), device_id_type=MESH)
    for way in range(2):
        @pl.when(z < 3 if way == 0 else z > 0)
        def _(way=way):
            pl.semaphore_signal(
                barrier, inc=1, device_id=(d, z + 1 - 2 * way), device_id_type=MESH
            )
    near = jnp.where((z == 0) | (z == 3), 1, 2)
    pl.semaphore_wait(barrier, 7 + near)

    pieces = 4
    hrows = rows // pieces

    def z_copy(block, h, way):
        span = slice(h * hrows, (h + 1) * hrows)
        return remote(
            zbuf.at[block, span], zbuf.at[block, span],
            zs.at[way, h, block], zr.at[h, block], d, z + 1 - 2 * way,
        )

    def z_send(h, way):
        @pl.when(z < 3 if way == 0 else z > 0)
        def _():
            z_copy(z, h, way).start()

    def z_pass(h):
        for t in range(1, 4):
            for way in range(2):
                block = z - t if way == 0 else z + t

                @pl.when(block >= 0 if way == 0 else block <= 3)
                def _(block=block, way=way):
                    z_copy(block, h, way).wait_recv()

                    @pl.when(z < 3 if way == 0 else z > 0)
                    def _():
                        z_copy(block, h, way).start()

                if h + 2 < pieces:
                    @pl.when(z == t if way == 0 else z == 3 - t)
                    def _(way=way):
                        z_send(h + 2, way)

    def z_drain():
        for h in range(pieces):
            for t in range(4):
                for way in range(2):
                    block = z - t if way == 0 else z + t

                    @pl.when((block >= 0) & (z < 3) if way == 0 else (block <= 3) & (z > 0))
                    def _(block=block, way=way, h=h):
                        z_copy(block, h, way).wait_send()

    zbuf[pl.ds(z, 1)] = x_ref[...][None]
    for way in range(2):
        z_send(0, way)
    for way in range(2):
        z_send(1, way)

        @pl.when(z == 0 if way == 0 else z == 3)
        def _(way=way):
            for h in range(2, pieces):
                z_send(h, way)

    t_copies = [
        remote(tscr, tabs.at[d], ts.at[o - 1], tr.at[o - 1], peer(o), z) for o in range(1, 8)
    ]
    for copy in t_copies:
        copy.start()
    tabs[pl.ds(d, 1)] = tscr[...][None]

    ro = lax.broadcasted_iota(jnp.int32, (cap, rows), 0)
    rj = lax.broadcasted_iota(jnp.int32, (cap, rows), 1)
    pick = jnp.concatenate(
        [
            jnp.where(
                (rj - ro == tscr[0:1, p:p + 1]) & (ro < tscr[1:2, p:p + 1]), 1.0, 0.0
            )
            for p in range(n_dp)
        ],
        axis=0,
    ).astype(BF)
    outr[...] = jnp.dot(
        pick, x_ref[...], preferred_element_type=F32
    ).astype(BF).reshape(n_dp, cap, feat)
    r_copies = [
        remote(outr.at[peer(o)], arr.at[d], rs.at[o - 1], rr.at[o - 1], peer(o), z)
        for o in (6, 7, 2, 3, 4, 5, 1)
    ]
    for copy in r_copies:
        copy.start()
    arr[pl.ds(d, 1)] = outr[pl.ds(d, 1)]

    step = 16
    total = float(feat * 4)

    def norm_rows(i, carry):
        span = pl.ds(pl.multiple_of(i * step, step), step)
        s1 = jnp.zeros((step, 1), F32)
        s2 = jnp.zeros((step, 1), F32)
        for b in range(4):
            v = zbuf[b, span, :].astype(F32)
            s1 += jnp.sum(v, axis=-1, keepdims=True)
            s2 += jnp.sum(v * v, axis=-1, keepdims=True)
        mid = s1 / total
        scale = lax.rsqrt(s2 / total - mid * mid + epsilon)
        for b in range(n_dp):
            lane = (b % 2) * kdim
            v = zbuf[b // 2, span, lane:lane + kdim].astype(F32)
            g = ng_ref[:, b * kdim:(b + 1) * kdim]
            nbuf[b, span, :] = ((v - mid) * scale * g).astype(BF)
        return carry

    a_copies = []
    for h in range(pieces):
        span = slice(h * hrows, (h + 1) * hrows)
        z_pass(h)
        lax.fori_loop(h * (hrows // step), (h + 1) * (hrows // step), norm_rows, 0)
        for o in (6, 7, 2, 3, 4, 5, 1):
            copy = remote(
                nbuf.at[peer(o), span], gbuf.at[d, span],
                asem.at[h, o - 1], ar.at[h, o - 1], peer(o), z,
            )
            copy.start()
            a_copies.append(copy)
    gbuf[pl.ds(d, 1)] = nbuf[pl.ds(d, 1)]

    for copy in t_copies:
        copy.wait_recv()
    pi = lax.broadcasted_iota(jnp.int32, (rows, rows), 0)
    pj = lax.broadcasted_iota(jnp.int32, (rows, rows), 1)
    delta = pi - pj
    for p in range(n_dp):
        spot = pl.multiple_of((p // 2 + 4 * (1 - (p % 2 + k) % 2)) * rows, rows)
        for s in range(n_dp):
            start = tabs[s, 0:1, p:p + 1]
            length = tabs[s, 1:2, p:p + 1]
            slot = tabs[p, 2:3, s:s + 1]
            hit = (delta == slot - start) & (pj >= start) & (pj < start + length)
            perm[pl.ds(spot, rows), s * rows:(s + 1) * rows] = jnp.where(hit, 1.0, 0.0).astype(BF)

    for copy in r_copies:
        copy.wait_recv()
    si = lax.broadcasted_iota(jnp.int32, (rows, cap), 0)
    so = lax.broadcasted_iota(jnp.int32, (rows, cap), 1)
    place = jnp.concatenate(
        [
            jnp.where(si - so == tscr[2:3, s:s + 1], 1.0, 0.0)
            for s in range(n_dp)
        ],
        axis=1,
    ).astype(BF)
    packed_ref[...] = jnp.dot(
        place, arr[...].reshape(n_dp * cap, feat), preferred_element_type=F32
    ).astype(BF)

    for copy in a_copies:
        copy.wait_recv()
    w_copy.wait()

    tile = 256

    def order_half(h):
        span = slice(h * half, (h + 1) * half)

        def body(t, carry):
            lane = pl.ds(pl.multiple_of(t * tile, tile), tile)
            right = gbuf[:, :, lane].reshape(n_dp * rows, tile)
            ordr[span, lane] = jnp.dot(
                perm[span, :], right, preferred_element_type=F32
            ).astype(BF)
            return carry

        lax.fori_loop(0, kdim // tile, body, 0)

    sibling = peer(1)
    s_copies = []
    c_copies = [[], [], []]

    def sibling_part(j):
        def body(t, carry):
            lane = pl.ds(pl.multiple_of(t * tile, tile), tile)
            sbuf[j, :, lane] = jnp.dot(
                ordr[:half, :], w_ref[j, :, lane], preferred_element_type=F32
            ).astype(BF)
            return carry

        lax.fori_loop(0, cols // tile, body, 0)
        copy = remote(sbuf.at[j], rbuf.at[j], ssem.at[j], sr.at[j], sibling, z)
        copy.start()
        s_copies.append(copy)

    def own_part(j):
        s_copies[j].wait_recv()

        def body(t, carry):
            lane = pl.ds(pl.multiple_of(t * tile, tile), tile)
            got = jnp.dot(ordr[half:, :], w_ref[j, :, lane], preferred_element_type=F32)
            got = (got + rbuf[j, :, lane].astype(F32)).astype(BF)
            cbuf[j, :, :, lane] = got.reshape(half // rows, rows, tile)
            return carry

        lax.fori_loop(0, cols // tile, body, 0)
        for oc in (3, 1, 2):
            copy = remote(
                cbuf.at[j, peer_chip(oc)], crecv.at[j, oc - 1],
                cs.at[j, oc - 1], cr.at[j, oc - 1], peer(2 * oc), z,
            )
            copy.start()
            c_copies[j].append(copy)

    order_half(0)
    sibling_part(0)
    order_half(1)
    sibling_part(1)
    own_part(0)
    sibling_part(2)
    own_part(1)
    own_part(2)

    hs = qg_ref.shape[1]
    heads = cols // hs
    chip = d // 2

    for j in range(3):
        for copy in c_copies[j]:
            copy.wait_recv()
        for h in range(heads):
            lane = slice(h * hs, (h + 1) * hs)
            v = cbuf[j, pl.ds(chip, 1), :, lane][0].astype(F32)
            for b in range(3):
                v += crecv[j, b, :, lane].astype(F32)
            if j < 2:
                mid = jnp.mean(v, axis=-1, keepdims=True)
                spread = jnp.mean(v * v, axis=-1, keepdims=True) - mid * mid
                gain = (qg_ref, kg_ref)[j][...]
                v = (v - mid) * lax.rsqrt(spread + epsilon) * gain
            (qn, kn, vn)[j][:, lane] = v.astype(BF)

    ids = jnp.broadcast_to(ids_ref[...], (rows, rows))
    same = ids == ids.T
    for h in range(heads):
        lane = slice(h * hs, (h + 1) * hs)
        scores = lax.dot_general(
            qn[:, lane], kn[:, lane], (((1,), (1,)), ((), ())), preferred_element_type=F32
        ) * hs ** (-0.5)
        raw = jnp.where(same, jnp.exp(scores), 0.0)
        att = (raw / jnp.sum(raw, axis=-1, keepdims=True)).astype(BF)
        ctx[:, lane] = jnp.dot(att, vn[:, lane], preferred_element_type=F32).astype(BF)

    ow_copy.wait()
    wide = 512

    def p_copy(m, way):
        return remote(
            psend.at[m], zrecv.at[way, m], ps.at[m], pr.at[way, m], d, z + 1 - 2 * way
        )

    for i in range(4):
        m = jnp.where(z < 2, 3 - i, i)

        def body(t, carry, m=m):
            lane = pl.ds(pl.multiple_of(t * wide, wide), wide)
            from_lane = pl.ds(pl.multiple_of(m * feat + t * wide, wide), wide)
            got = jnp.dot(ctx[...], ow_ref[:, from_lane], preferred_element_type=F32)
            pbuf[m, :, lane] = got.astype(BF)
            return carry

        lax.fori_loop(0, feat // wide, body, 0)

        for way, end in ((0, 0), (1, 3)):
            if i < 3:
                @pl.when(z == end)
                def _(m=3 - i if end == 0 else i, way=way):
                    psend[m] = pbuf[m]
                    p_copy(m, way).start()

    for at, m in ((1, 3), (2, 0), (1, 2), (2, 1), (2, 3), (1, 0)):
        way = 0 if m > at else 1

        @pl.when(z == at)
        def _(m=m, way=way):
            p_copy(m, way).wait_recv()
            psend[m] = (pbuf[m].astype(F32) + zrecv[way, m].astype(F32)).astype(BF)
            p_copy(m, way).start()

    for way, end in ((0, 0), (1, 3)):
        @pl.when(z != end)
        def _(way=way):
            p_copy(z, way).wait_recv()

    mine = pbuf[pl.ds(z, 1)][0].astype(F32)

    @pl.when(z == 0)
    def _():
        out_ref[...] = (mine + zrecv[1, 0].astype(F32)).astype(BF)

    @pl.when(z == 3)
    def _():
        out_ref[...] = (mine + zrecv[0, 3].astype(F32)).astype(BF)

    for at in (1, 2):
        @pl.when(z == at)
        def _(at=at):
            both = zrecv[0, at].astype(F32) + zrecv[1, at].astype(F32)
            out_ref[...] = (mine + both).astype(BF)

    for m in range(4):
        @pl.when(z < m)
        def _(m=m):
            p_copy(m, 0).wait_send()

        @pl.when(z > m)
        def _(m=m):
            p_copy(m, 1).wait_send()

    for copy in t_copies + r_copies + a_copies + s_copies + sum(c_copies, []):
        copy.wait_send()
    z_drain()


def fused_on_device(
    patches,
    send_start,
    run_length,
    slot_start,
    image_ids,
    norm_gain,
    qkv_weight,
    query_gain,
    key_gain,
    out_weight,
):
    rows, feat = patches.shape
    n_dp = lax.axis_size("dp")
    n_mp = lax.axis_size("mp")
    cap = 2 * rows // n_dp
    kdim, _, cols = qkv_weight.shape
    width = out_weight.shape[1]
    half = n_dp // 2 * rows
    weight = jnp.transpose(qkv_weight, (1, 0, 2))
    vm = pl.BlockSpec(memory_space=pltpu.VMEM)
    hbm = pl.BlockSpec(memory_space=pl.ANY)
    dma = pltpu.SemaphoreType.DMA
    return pl.pallas_call(
        fused_kernel,
        out_shape=(
            jax.ShapeDtypeStruct((rows, feat), BF),
            jax.ShapeDtypeStruct((rows, feat), BF),
        ),
        in_specs=[vm] * 8 + [hbm] * 2,
        out_specs=(vm, vm),
        scratch_shapes=[
            pltpu.VMEM((3, kdim, cols), BF),
            pltpu.VMEM((cols, width), BF),
            pltpu.VMEM((n_mp, rows, feat), BF),
            pltpu.VMEM((n_dp, rows, kdim), BF),
            pltpu.VMEM((n_dp, rows, kdim), BF),
            pltpu.VMEM((n_dp, cap, feat), BF),
            pltpu.VMEM((n_dp, cap, feat), BF),
            pltpu.VMEM((8, 128), jnp.int32),
            pltpu.VMEM((n_dp, 8, 128), jnp.int32),
            pltpu.VMEM((2 * half, 2 * half), BF),
            pltpu.VMEM((2 * half, kdim), BF),
            pltpu.VMEM((3, half, cols), BF),
            pltpu.VMEM((3, half, cols), BF),
            pltpu.VMEM((3, n_dp // 2, rows, cols), BF),
            pltpu.VMEM((3, n_dp // 2 - 1, rows, cols), BF),
            pltpu.VMEM((rows, cols), BF),
            pltpu.VMEM((rows, cols), BF),
            pltpu.VMEM((rows, cols), BF),
            pltpu.VMEM((rows, cols), BF),
            pltpu.VMEM((n_mp, rows, feat), BF),
            pltpu.VMEM((n_mp, rows, feat), BF),
            pltpu.VMEM((2, n_mp, rows, feat), BF),
            dma((2,)),
            dma((2, 4, n_mp)), dma((4, n_mp)),
            dma((4, 7)), dma((4, 7)),
            dma((7,)), dma((7,)),
            dma((7,)), dma((7,)),
            dma((3,)), dma((3,)),
            dma((3, 3)), dma((3, 3)),
            dma((n_mp,)), dma((2, n_mp)),
        ],
        compiler_params=pltpu.CompilerParams(
            collective_id=0, has_side_effects=True, vmem_limit_bytes=60 * 1024 * 1024
        ),
    )(
        patches, send_start, run_length, slot_start, image_ids,
        norm_gain.reshape(1, -1), query_gain.reshape(1, -1), key_gain.reshape(1, -1),
        weight, out_weight,
    )


def solution(mesh):
    small = mesh.shape["dp"] == 8 and mesh.shape["mp"] == 4
    return jax.shard_map(
        fused_on_device if small else plain_on_device,
        mesh=mesh,
        in_specs=(
            P("dp", "mp"),
            P("dp", None),
            P("dp", None),
            P("dp", None),
            P("dp", None),
            P(),
            P("dp", None, "mp"),
            P(),
            P(),
            P("mp", None),
        ),
        out_specs=(P("dp", "mp"), P("dp", "mp")),
        check_vma=False,
    )
```

```python
import functools

import jax
import jax.numpy as jnp
from jax import lax
from jax.experimental import pallas as pl
from jax.experimental.pallas import tpu as pltpu
from jax.sharding import PartitionSpec as P

epsilon = 1e-06


def row_norm(values, scales):
    middle = jnp.mean(values, axis=-1, keepdims=True)
    spread = jnp.mean(values * values, axis=-1, keepdims=True) - middle * middle
    return (values - middle) * lax.rsqrt(spread + epsilon) * scales


def plain_on_device(
    patches,
    send_start,
    run_length,
    slot_start,
    image_ids,
    norm_gain,
    qkv_weight,
    query_gain,
    key_gain,
    out_weight,
):
    pack_rows, feat_local = patches.shape
    pack_count = lax.axis_size("dp")
    mp_count = lax.axis_size("mp")
    capacity = 2 * pack_rows // pack_count
    local_cols = qkv_weight.shape[1] * qkv_weight.shape[2]
    offsets = jnp.arange(capacity, dtype=jnp.int32)
    rows = jnp.arange(pack_rows, dtype=jnp.int32)

    x = patches.astype(jnp.float32)
    sums = jnp.stack([jnp.sum(x, axis=-1), jnp.sum(x * x, axis=-1)])
    sums = lax.psum(sums, "mp") / (feat_local * mp_count)
    middle = sums[0][:, None]
    spread = sums[1][:, None] - middle * middle
    gain = lax.dynamic_slice_in_dim(norm_gain, lax.axis_index("mp") * feat_local, feat_local)
    normed = ((x - middle) * lax.rsqrt(spread + epsilon) * gain).astype(jnp.bfloat16)

    wide = lax.all_gather(normed, "mp", axis=1, tiled=True)
    slices = lax.all_to_all(wide, "dp", split_axis=1, concat_axis=0, tiled=True)

    tables = jnp.concatenate([send_start, run_length, slot_start], axis=0)[None]
    tables = lax.all_gather(tables, "dp", axis=0, tiled=True)
    starts, lengths, slots = tables[:, 0].T, tables[:, 1].T, tables[:, 2]
    inside = (rows >= slots[:, :, None]) & (rows < (slots + lengths)[:, :, None])
    base = jnp.arange(pack_count, dtype=jnp.int32)[None, :] * pack_rows + starts - slots
    origin = jnp.sum(jnp.where(inside, base[:, :, None] + rows, 0), axis=1).reshape(-1)
    chosen = (origin[:, None] == jnp.arange(origin.shape[0], dtype=jnp.int32)).astype(jnp.bfloat16)
    ordered = jnp.dot(chosen, slices, preferred_element_type=jnp.float32).astype(jnp.bfloat16)

    partial = jnp.dot(
        ordered, qkv_weight.reshape(qkv_weight.shape[0], local_cols), preferred_element_type=jnp.float32
    ).astype(jnp.bfloat16)
    projected = lax.psum_scatter(partial, "dp", scatter_dimension=0, tiled=True).astype(jnp.float32)

    own_rows = send_start[0][:, None] + offsets[None, :]
    occupied = offsets[None, :] < run_length[0][:, None]
    pick = (occupied[:, :, None] & (own_rows[:, :, None] == rows)).astype(jnp.bfloat16)
    outgoing = jnp.dot(
        pick.reshape(-1, pack_rows), patches, preferred_element_type=jnp.float32
    ).astype(jnp.bfloat16)
    arrived = lax.all_to_all(
        outgoing.reshape(pack_count, capacity, feat_local), "dp", split_axis=0, concat_axis=0, tiled=True
    )
    targets = (slot_start[0][:, None] + offsets[None, :]).reshape(-1)
    place = (rows[:, None] == targets[None, :]).astype(jnp.bfloat16)
    packed = jnp.dot(
        place, arrived.reshape(-1, feat_local), preferred_element_type=jnp.float32
    ).astype(jnp.bfloat16)

    head_size = query_gain.shape[0]
    heads_here = qkv_weight.shape[2] // head_size
    split_heads = projected.reshape(pack_rows, 3, heads_here, head_size)
    queries = row_norm(split_heads[:, 0], query_gain).astype(jnp.bfloat16)
    key_rows = row_norm(split_heads[:, 1], key_gain).astype(jnp.bfloat16)
    values = split_heads[:, 2].astype(jnp.bfloat16)
    scores = jnp.einsum(
        "qhd,khd->hqk", queries, key_rows, preferred_element_type=jnp.float32
    ) * head_size ** (-0.5)
    image_of = image_ids[0]
    same_image = image_of[:, None] == image_of[None, :]
    weights_raw = jnp.where(same_image[None], jnp.exp(scores), 0.0)
    totals = jnp.sum(weights_raw, axis=-1, keepdims=True)
    attention = (weights_raw / totals).astype(jnp.bfloat16)
    context = jnp.einsum(
        "hqk,khd->qhd", attention, values, preferred_element_type=jnp.float32
    ).astype(jnp.bfloat16)
    context = context.reshape(pack_rows, heads_here * head_size)
    partial_value = jnp.dot(context, out_weight, preferred_element_type=jnp.float32)
    attended = lax.psum_scatter(
        partial_value.astype(jnp.bfloat16), "mp", scatter_dimension=1, tiled=True
    )
    return (packed, attended)


MESH = pl.DeviceIdType.MESH
BF = jnp.bfloat16
F32 = jnp.float32


def fused_kernel(
    x_ref, ss_ref, rl_ref, sl_ref, ids_ref, ng_ref, qg_ref, kg_ref, w_hbm, ow_hbm,
    packed_ref, out_ref,
    w_ref, ow_ref, zbuf, nbuf, gbuf, outr, arr, tscr, tabs, perm, ordr,
    sbuf, rbuf, cbuf, crecv, fbuf, frecv, qn, kn, vn, ctx, pbuf, psend, zrecv,
    w_sem, zs, zr, asem, ar, rs, rr, ts, tr, ssem, sr, cs, cr, fs, fr, ps, pr,
):
    rows, feat = x_ref.shape
    n_dp, cap = outr.shape[0], outr.shape[1]
    kdim, cols = w_ref.shape[1], w_ref.shape[2]
    half = n_dp // 2 * rows
    d = lax.axis_index("dp")
    z = lax.axis_index("mp")
    k = d % 2
    cx = (d // 2) % 2
    cy = d // 4

    def peer_chip(oc):
        return ((cy + oc // 2) % 2) * 2 + (cx + oc % 2) % 2

    def peer(o):
        return peer_chip(o // 2) * 2 + (k + o % 2) % 2

    def remote(src, dst, s, r, dd, zz):
        return pltpu.make_async_remote_copy(
            src_ref=src, dst_ref=dst, send_sem=s, recv_sem=r,
            device_id=(dd, zz), device_id_type=MESH,
        )

    w_copy = pltpu.make_async_copy(w_hbm, w_ref, w_sem.at[0])
    ow_copy = pltpu.make_async_copy(ow_hbm, ow_ref, w_sem.at[1])
    w_copy.start()
    ow_copy.start()

    tscr[...] = jnp.zeros_like(tscr)
    tscr[0:1, 0:n_dp] = ss_ref[...]
    tscr[1:2, 0:n_dp] = rl_ref[...]
    tscr[2:3, 0:n_dp] = sl_ref[...]

    barrier = pltpu.get_barrier_semaphore()
    for o in range(1, 8):
        pl.semaphore_signal(barrier, inc=1, device_id=(peer(o), z), device_id_type=MESH)
    for way in range(2):
        @pl.when(z < 3 if way == 0 else z > 0)
        def _(way=way):
            pl.semaphore_signal(
                barrier, inc=1, device_id=(d, z + 1 - 2 * way), device_id_type=MESH
            )
    near = jnp.where((z == 0) | (z == 3), 1, 2)
    pl.semaphore_wait(barrier, 7 + near)

    pieces = 4
    hrows = rows // pieces

    def z_copy(block, h, way):
        span = slice(h * hrows, (h + 1) * hrows)
        return remote(
            zbuf.at[block, span], zbuf.at[block, span],
            zs.at[way, h, block], zr.at[h, block], d, z + 1 - 2 * way,
        )

    def z_send(h, way):
        @pl.when(z < 3 if way == 0 else z > 0)
        def _():
            z_copy(z, h, way).start()

    def z_pass(h):
        for t in range(1, 4):
            for way in range(2):
                block = z - t if way == 0 else z + t

                @pl.when(block >= 0 if way == 0 else block <= 3)
                def _(block=block, way=way):
                    z_copy(block, h, way).wait_recv()

                    @pl.when(z < 3 if way == 0 else z > 0)
                    def _():
                        z_copy(block, h, way).start()

                if h + 2 < pieces:
                    @pl.when(z == t if way == 0 else z == 3 - t)
                    def _(way=way):
                        z_send(h + 2, way)

    def z_drain():
        for h in range(pieces):
            for t in range(4):
                for way in range(2):
                    block = z - t if way == 0 else z + t

                    @pl.when((block >= 0) & (z < 3) if way == 0 else (block <= 3) & (z > 0))
                    def _(block=block, way=way, h=h):
                        z_copy(block, h, way).wait_send()

    zbuf[pl.ds(z, 1)] = x_ref[...][None]
    for way in range(2):
        z_send(0, way)
    for way in range(2):
        z_send(1, way)

        @pl.when(z == 0 if way == 0 else z == 3)
        def _(way=way):
            for h in range(2, pieces):
                z_send(h, way)

    t_copies = [
        remote(tscr, tabs.at[d], ts.at[o - 1], tr.at[o - 1], peer(o), z) for o in range(1, 8)
    ]
    for copy in t_copies:
        copy.start()
    tabs[pl.ds(d, 1)] = tscr[...][None]

    ro = lax.broadcasted_iota(jnp.int32, (cap, rows), 0)
    rj = lax.broadcasted_iota(jnp.int32, (cap, rows), 1)
    pick = jnp.concatenate(
        [
            jnp.where(
                (rj - ro == tscr[0:1, p:p + 1]) & (ro < tscr[1:2, p:p + 1]), 1.0, 0.0
            )
            for p in range(n_dp)
        ],
        axis=0,
    ).astype(BF)
    outr[...] = jnp.dot(
        pick, x_ref[...], preferred_element_type=F32
    ).astype(BF).reshape(n_dp, cap, feat)
    r_copies = [
        remote(outr.at[peer(o)], arr.at[d], rs.at[o - 1], rr.at[o - 1], peer(o), z)
        for o in (6, 7, 2, 3, 4, 5, 1)
    ]
    for copy in r_copies:
        copy.start()
    arr[pl.ds(d, 1)] = outr[pl.ds(d, 1)]

    step = 16
    total = float(feat * 4)

    def norm_rows(i, carry):
        span = pl.ds(pl.multiple_of(i * step, step), step)
        s1 = jnp.zeros((step, 1), F32)
        s2 = jnp.zeros((step, 1), F32)
        for b in range(4):
            v = zbuf[b, span, :].astype(F32)
            s1 += jnp.sum(v, axis=-1, keepdims=True)
            s2 += jnp.sum(v * v, axis=-1, keepdims=True)
        mid = s1 / total
        scale = lax.rsqrt(s2 / total - mid * mid + epsilon)
        for b in range(n_dp):
            lane = (b % 2) * kdim
            v = zbuf[b // 2, span, lane:lane + kdim].astype(F32)
            g = ng_ref[:, b * kdim:(b + 1) * kdim]
            nbuf[b, span, :] = ((v - mid) * scale * g).astype(BF)
        return carry

    a_copies = []
    for h in range(pieces):
        span = slice(h * hrows, (h + 1) * hrows)
        z_pass(h)
        lax.fori_loop(h * (hrows // step), (h + 1) * (hrows // step), norm_rows, 0)
        for o in (6, 7, 2, 3, 4, 5, 1):
            copy = remote(
                nbuf.at[peer(o), span], gbuf.at[d, span],
                asem.at[h, o - 1], ar.at[h, o - 1], peer(o), z,
            )
            copy.start()
            a_copies.append(copy)
    gbuf[pl.ds(d, 1)] = nbuf[pl.ds(d, 1)]

    for copy in t_copies:
        copy.wait_recv()
    pi = lax.broadcasted_iota(jnp.int32, (rows, rows), 0)
    pj = lax.broadcasted_iota(jnp.int32, (rows, rows), 1)
    delta = pi - pj
    for p in range(n_dp):
        spot = pl.multiple_of((p // 2 + 4 * (1 - (p % 2 + k) % 2)) * rows, rows)
        for s in range(n_dp):
            start = tabs[s, 0:1, p:p + 1]
            length = tabs[s, 1:2, p:p + 1]
            slot = tabs[p, 2:3, s:s + 1]
            hit = (delta == slot - start) & (pj >= start) & (pj < start + length)
            perm[pl.ds(spot, rows), s * rows:(s + 1) * rows] = jnp.where(hit, 1.0, 0.0).astype(BF)

    for copy in r_copies:
        copy.wait_recv()
    si = lax.broadcasted_iota(jnp.int32, (rows, cap), 0)
    so = lax.broadcasted_iota(jnp.int32, (rows, cap), 1)
    place = jnp.concatenate(
        [
            jnp.where(si - so == tscr[2:3, s:s + 1], 1.0, 0.0)
            for s in range(n_dp)
        ],
        axis=1,
    ).astype(BF)
    packed_ref[...] = jnp.dot(
        place, arr[...].reshape(n_dp * cap, feat), preferred_element_type=F32
    ).astype(BF)

    for copy in a_copies:
        copy.wait_recv()
    w_copy.wait()

    tile = 256

    def order_half(h):
        span = slice(h * half, (h + 1) * half)

        def body(t, carry):
            lane = pl.ds(pl.multiple_of(t * tile, tile), tile)
            right = gbuf[:, :, lane].reshape(n_dp * rows, tile)
            ordr[span, lane] = jnp.dot(
                perm[span, :], right, preferred_element_type=F32
            ).astype(BF)
            return carry

        lax.fori_loop(0, kdim // tile, body, 0)

    sibling = peer(1)
    s_copies = []
    c_copies = [[], [], []]
    f_copies = [[], [], []]
    part = cols // 2

    def sibling_part(j):
        def body(t, carry):
            lane = pl.ds(pl.multiple_of(t * tile, tile), tile)
            sbuf[j, :, lane] = jnp.dot(
                ordr[:half, :], w_ref[j, :, lane], preferred_element_type=F32
            ).astype(BF)
            return carry

        lax.fori_loop(0, cols // tile, body, 0)
        copy = remote(sbuf.at[j], rbuf.at[j], ssem.at[j], sr.at[j], sibling, z)
        copy.start()
        s_copies.append(copy)

    def own_part(j):
        s_copies[j].wait_recv()

        def body(t, carry):
            lane = pl.ds(pl.multiple_of(t * tile, tile), tile)
            got = jnp.dot(ordr[half:, :], w_ref[j, :, lane], preferred_element_type=F32)
            got = (got + rbuf[j, :, lane].astype(F32)).astype(BF)
            cbuf[j, :, :, lane] = got.reshape(half // rows, rows, tile)
            return carry

        lax.fori_loop(0, cols // tile, body, 0)
        for slot in (1, 0):
            for first in (1, 2):
                goal = peer_chip(3) if slot else peer_chip(first)
                copy = remote(
                    cbuf.at[j, goal, :, (first - 1) * part:first * part],
                    crecv.at[j, first - 1, slot],
                    cs.at[j, first - 1, slot], cr.at[j, first - 1, slot], peer(2 * first), z,
                )
                copy.start()
                c_copies[j].append(copy)

    def pass_on(j):
        for first in (1, 2):
            c_copies[j][first - 1].wait_recv()
            own = cbuf[j, pl.ds(peer_chip(3 - first), 1), :, (first - 1) * part:first * part][0]
            both = own.astype(F32) + crecv[j, first - 1, 1].astype(F32)
            fbuf[j, first - 1] = both.astype(BF)
            copy = remote(
                fbuf.at[j, first - 1], frecv.at[j, first - 1],
                fs.at[j, first - 1], fr.at[j, first - 1], peer(2 * (3 - first)), z,
            )
            copy.start()
            f_copies[j].append(copy)

    order_half(0)
    sibling_part(0)
    order_half(1)
    sibling_part(1)
    own_part(0)
    sibling_part(2)
    own_part(1)
    pass_on(0)
    own_part(2)
    pass_on(1)
    pass_on(2)

    hs = qg_ref.shape[1]
    heads = cols // hs
    chip = d // 2

    for j in range(3):
        for copy in c_copies[j][2:] + f_copies[j]:
            copy.wait_recv()
        for h in range(heads):
            lane = slice(h * hs, (h + 1) * hs)
            v = cbuf[j, pl.ds(chip, 1), :, lane][0].astype(F32)
            way = h * hs // part
            near = slice(h * hs - way * part, (h + 1) * hs - way * part)
            v += crecv[j, way, 0, :, near].astype(F32) + frecv[j, way, :, near].astype(F32)
            if j < 2:
                mid = jnp.mean(v, axis=-1, keepdims=True)
                spread = jnp.mean(v * v, axis=-1, keepdims=True) - mid * mid
                gain = (qg_ref, kg_ref)[j][...]
                v = (v - mid) * lax.rsqrt(spread + epsilon) * gain
            (qn, kn, vn)[j][:, lane] = v.astype(BF)

    ids = jnp.broadcast_to(ids_ref[...], (rows, rows))
    same = ids == ids.T
    for h in range(heads):
        lane = slice(h * hs, (h + 1) * hs)
        scores = lax.dot_general(
            qn[:, lane], kn[:, lane], (((1,), (1,)), ((), ())), preferred_element_type=F32
        ) * hs ** (-0.5)
        raw = jnp.where(same, jnp.exp(scores), 0.0)
        att = (raw / jnp.sum(raw, axis=-1, keepdims=True)).astype(BF)
        ctx[:, lane] = jnp.dot(att, vn[:, lane], preferred_element_type=F32).astype(BF)

    ow_copy.wait()
    wide = 512

    def p_copy(m, way):
        return remote(
            psend.at[m], zrecv.at[way, m], ps.at[m], pr.at[way, m], d, z + 1 - 2 * way
        )

    for i in range(4):
        m = jnp.where(z < 2, 3 - i, i)

        def body(t, carry, m=m):
            lane = pl.ds(pl.multiple_of(t * wide, wide), wide)
            from_lane = pl.ds(pl.multiple_of(m * feat + t * wide, wide), wide)
            got = jnp.dot(ctx[...], ow_ref[:, from_lane], preferred_element_type=F32)
            pbuf[m, :, lane] = got.astype(BF)
            return carry

        lax.fori_loop(0, feat // wide, body, 0)

        for way, end in ((0, 0), (1, 3)):
            if i < 3:
                @pl.when(z == end)
                def _(m=3 - i if end == 0 else i, way=way):
                    psend[m] = pbuf[m]
                    p_copy(m, way).start()

    for at, m in ((1, 3), (2, 0), (1, 2), (2, 1), (2, 3), (1, 0)):
        way = 0 if m > at else 1

        @pl.when(z == at)
        def _(m=m, way=way):
            p_copy(m, way).wait_recv()
            psend[m] = (pbuf[m].astype(F32) + zrecv[way, m].astype(F32)).astype(BF)
            p_copy(m, way).start()

    for way, end in ((0, 0), (1, 3)):
        @pl.when(z != end)
        def _(way=way):
            p_copy(z, way).wait_recv()

    mine = pbuf[pl.ds(z, 1)][0].astype(F32)

    @pl.when(z == 0)
    def _():
        out_ref[...] = (mine + zrecv[1, 0].astype(F32)).astype(BF)

    @pl.when(z == 3)
    def _():
        out_ref[...] = (mine + zrecv[0, 3].astype(F32)).astype(BF)

    for at in (1, 2):
        @pl.when(z == at)
        def _(at=at):
            both = zrecv[0, at].astype(F32) + zrecv[1, at].astype(F32)
            out_ref[...] = (mine + both).astype(BF)

    for m in range(4):
        @pl.when(z < m)
        def _(m=m):
            p_copy(m, 0).wait_send()

        @pl.when(z > m)
        def _(m=m):
            p_copy(m, 1).wait_send()

    for copy in t_copies + r_copies + a_copies + s_copies + sum(c_copies + f_copies, []):
        copy.wait_send()
    z_drain()


def fused_on_device(
    patches,
    send_start,
    run_length,
    slot_start,
    image_ids,
    norm_gain,
    qkv_weight,
    query_gain,
    key_gain,
    out_weight,
):
    rows, feat = patches.shape
    n_dp = lax.axis_size("dp")
    n_mp = lax.axis_size("mp")
    cap = 2 * rows // n_dp
    kdim, _, cols = qkv_weight.shape
    width = out_weight.shape[1]
    half = n_dp // 2 * rows
    weight = jnp.transpose(qkv_weight, (1, 0, 2))
    vm = pl.BlockSpec(memory_space=pltpu.VMEM)
    hbm = pl.BlockSpec(memory_space=pl.ANY)
    dma = pltpu.SemaphoreType.DMA
    return pl.pallas_call(
        fused_kernel,
        out_shape=(
            jax.ShapeDtypeStruct((rows, feat), BF),
            jax.ShapeDtypeStruct((rows, feat), BF),
        ),
        in_specs=[vm] * 8 + [hbm] * 2,
        out_specs=(vm, vm),
        scratch_shapes=[
            pltpu.VMEM((3, kdim, cols), BF),
            pltpu.VMEM((cols, width), BF),
            pltpu.VMEM((n_mp, rows, feat), BF),
            pltpu.VMEM((n_dp, rows, kdim), BF),
            pltpu.VMEM((n_dp, rows, kdim), BF),
            pltpu.VMEM((n_dp, cap, feat), BF),
            pltpu.VMEM((n_dp, cap, feat), BF),
            pltpu.VMEM((8, 128), jnp.int32),
            pltpu.VMEM((n_dp, 8, 128), jnp.int32),
            pltpu.VMEM((2 * half, 2 * half), BF),
            pltpu.VMEM((2 * half, kdim), BF),
            pltpu.VMEM((3, half, cols), BF),
            pltpu.VMEM((3, half, cols), BF),
            pltpu.VMEM((3, n_dp // 2, rows, cols), BF),
            pltpu.VMEM((3, 2, 2, rows, cols // 2), BF),
            pltpu.VMEM((3, 2, rows, cols // 2), BF),
            pltpu.VMEM((3, 2, rows, cols // 2), BF),
            pltpu.VMEM((rows, cols), BF),
            pltpu.VMEM((rows, cols), BF),
            pltpu.VMEM((rows, cols), BF),
            pltpu.VMEM((rows, cols), BF),
            pltpu.VMEM((n_mp, rows, feat), BF),
            pltpu.VMEM((n_mp, rows, feat), BF),
            pltpu.VMEM((2, n_mp, rows, feat), BF),
            dma((2,)),
            dma((2, 4, n_mp)), dma((4, n_mp)),
            dma((4, 7)), dma((4, 7)),
            dma((7,)), dma((7,)),
            dma((7,)), dma((7,)),
            dma((3,)), dma((3,)),
            dma((3, 2, 2)), dma((3, 2, 2)),
            dma((3, 2)), dma((3, 2)),
            dma((n_mp,)), dma((2, n_mp)),
        ],
        compiler_params=pltpu.CompilerParams(
            collective_id=0, has_side_effects=True, vmem_limit_bytes=60 * 1024 * 1024
        ),
    )(
        patches, send_start, run_length, slot_start, image_ids,
        norm_gain.reshape(1, -1), query_gain.reshape(1, -1), key_gain.reshape(1, -1),
        weight, out_weight,
    )


def solution(mesh):
    small = mesh.shape["dp"] == 8 and mesh.shape["mp"] == 4
    return jax.shard_map(
        fused_on_device if small else plain_on_device,
        mesh=mesh,
        in_specs=(
            P("dp", "mp"),
            P("dp", None),
            P("dp", None),
            P("dp", None),
            P("dp", None),
            P(),
            P("dp", None, "mp"),
            P(),
            P(),
            P("mp", None),
        ),
        out_specs=(P("dp", "mp"), P("dp", "mp")),
        check_vma=False,
    )
```
